512 devices in a mesh: blk: 8 (over y_lo, core), leaf: 64 (over z, y_hi, x).
Axes of the slice: x: 4, y: 8 (y_hi: 2, y_lo: 4; y = y_hi * 4 + y_lo), z: 8, core: 2. Of those that a mesh axis runs over, the one named last changes fastest.
Arguments:
- positions: float32 [3, 64, 8, 128], P(None, 'leaf', 'blk'), may hold values from 0 to 32, as said below
- panel_areas: float32 [64, 8, 128], P('leaf', 'blk'), may hold values from 0.5 to 2
- probe_cols: bfloat16 [576, 64, 8, 128], P(None, 'leaf', 'blk'), may hold values from -5 to 5
- full_sketch: bfloat16 [576, 64, 8, 128], P(None, 'leaf', 'blk'), may hold values from -3 to 3
- tree_order: int32 [64, 8, 128], P('leaf', 'blk'), may hold values from 0 to 127, each once within a row
- leaf_basis: bfloat16 [64, 8, 128, 512], P('leaf', 'blk'), may hold values from -0.1875 to 0.1875
- transfer_mats: bfloat16 [64, 3, 512, 512], P('leaf'), may hold values from -0.1875 to 0.1875
Outputs:
- offdiag_sketch: bfloat16 [576, 64, 8, 128], P(None, 'leaf', 'blk')
- nested_sketch: float32 [64, 2, 576, 512], P('leaf')
The draws below stay inside these ranges and needn't reach their ends.
Inputs may be any that keep to these rules, and one draw needn't show every extreme that they name: `positions`: each leaf's panel centres lie on a surface patch of 32 by 32 mean panel widths. `tree_order`: along the last dimension, each row names every one of the 128 panels of its block once.
All inputs are finite; a program needn't handle non-finite values.
Results may differ from the reference program's by a relative error of at most 0.0046.
Values sent between devices are 32-bit elements; how exact they have to be, the bound alone decides.
No kernel may reach another device: no remote copies, remote signals or barrier semaphores. Data moves between devices by JAX's collectives and lax.ppermute only.
A program may use at most 64 MiB of HBM per device.

```python
import math
import jax
import jax.numpy as jnp
from jax import lax

GRID = 32
R = 576
Q = 512
LEVELS = 3
P_DEV = 128
NODES = 64
BLOCKS = 8
N_BLK = 8


def draw_positions(key, part):
    cell_count = BLOCKS * P_DEV
    key_list = jax.random.split(key, 4)
    leaf_keys = jax.random.split(key_list[0], NODES)
    counting = jnp.broadcast_to(jnp.arange(cell_count, dtype=jnp.int32), (NODES, cell_count))
    cell_order = jax.vmap(jax.random.permutation)(leaf_keys, counting)
    column = cell_order % GRID
    row_index = cell_order // GRID
    jitter = jax.random.uniform(key_list[1], (2, NODES, cell_count), jnp.float32, -0.5, 0.5)
    roughness = jax.random.uniform(key_list[2], (NODES, cell_count), jnp.float32, 0.0, 0.5)
    height = jax.random.randint(key_list[3], (NODES, cell_count), 0, 2).astype(jnp.float32) + roughness
    first_coord = column.astype(jnp.float32) + 0.5 + jitter[0]
    second_coord = row_index.astype(jnp.float32) + 0.5 + jitter[1]
    stacked = jnp.stack([first_coord, second_coord, height], axis=0)
    return stacked.reshape(3, NODES, BLOCKS, P_DEV)


def level_of(key, shape, shards, least, largest):
    loudness, own = 1.0, jax.random.fold_in(key, 6)
    for position, blocks in shards:
        draws = jnp.exp(jax.random.uniform(jax.random.fold_in(own, position), (blocks,), jnp.float32, least / len(shards), largest / len(shards)))
        loudness = loudness * jnp.repeat(draws, shape[position] // blocks).reshape([-1 if axis == position else 1 for axis in range(len(shape))])
    return loudness


def scatter_about(own_key, extent, scale, most, pieces=(), kind=jnp.bfloat16):
    array = jax.random.normal(own_key, extent, jnp.float32) * scale
    if len(pieces) > 0:
        array = level_of(own_key, extent, pieces, -0.22, 0.18) * array
    return jnp.clip(array, min=-most, max=most).astype(kind)


def setup_inputs(seed: int = 0) -> dict:
    splits = jax.random.split(jax.random.key(seed), 8)
    positions = draw_positions(jax.random.fold_in(splits[7], 71), 0)
    panel_areas = jnp.clip(jnp.exp(math.log(2.0) - 1.3862944 * jax.random.uniform(splits[1], (NODES, BLOCKS, P_DEV), jnp.float32) ** level_of(splits[1], (NODES, BLOCKS, P_DEV), ((0, 64), (1, 8)), -0.2, 0.2)), 0.5, 2.0)
    probe_cols = scatter_about(splits[2], (R, NODES, BLOCKS, P_DEV), 1.0, 5.0, ((1, 64), (2, 8)))
    full_sketch = scatter_about(splits[3], (R, NODES, BLOCKS, P_DEV), 0.5, 3.0, ((1, 64), (2, 8)))
    tree_order = jax.vmap(lambda own: jax.random.permutation(own, P_DEV))(jax.random.split(splits[4], NODES * BLOCKS)).reshape((NODES, BLOCKS, P_DEV)).astype(jnp.int32)
    leaf_basis = scatter_about(splits[5], (NODES, BLOCKS, P_DEV, Q), (N_BLK * P_DEV) ** -0.5, 0.1875, ((0, 64), (1, 8)))
    transfer_mats = scatter_about(splits[6], (NODES, LEVELS, Q, Q), (2 * Q) ** -0.5, 0.1875, ((0, 64),))
    return {"positions": positions, "panel_areas": panel_areas, "probe_cols": probe_cols, "full_sketch": full_sketch, "tree_order": tree_order, "leaf_basis": leaf_basis, "transfer_mats": transfer_mats}


inv_four_pi = 1.0 / (4.0 * math.pi)

def kernel_tile(target_pos, target_area, source_pos, source_area):
    distance = jnp.zeros((target_pos.shape[1], source_pos.shape[1]), jnp.float32)
    for component in range(3):
        gap = target_pos[component][:, None] - source_pos[component][None, :]
        distance = distance + gap * gap
    soft = distance + 0.5 * (target_area[:, None] + source_area[None, :])
    return (inv_four_pi * lax.rsqrt(soft)).astype(jnp.bfloat16)

def reference(positions, panel_areas, probe_cols, full_sketch, tree_order, leaf_basis, transfer_mats):
    node_count = positions.shape[1]
    block_total = positions.shape[2]
    panels = positions.shape[3]
    probe_count = probe_cols.shape[0]
    block_size = min(512, panels)
    scaled = (panel_areas[None].astype(jnp.float32) * probe_cols.astype(jnp.float32)).astype(jnp.bfloat16)

    def leaf_near(items):
        leaf_pos, leaf_area, leaf_scaled = items
        source_pos = leaf_pos.reshape(3, -1)
        source_area = leaf_area.reshape(-1)
        source_scaled = leaf_scaled.reshape(probe_count, -1)
        block_count = source_pos.shape[1] // block_size
        target_blocks = jnp.transpose(source_pos.reshape(3, block_count, block_size), (1, 0, 2))
        area_blocks = source_area.reshape(block_count, block_size)

        def one_block(entry):
            block_pos, block_area = entry
            kernel = kernel_tile(block_pos, block_area, source_pos, source_area)
            return lax.dot_general(source_scaled, kernel, (((1,), (1,)), ((), ())), preferred_element_type=jnp.float32)
        sums = lax.map(one_block, (target_blocks, area_blocks))
        return jnp.transpose(sums, (1, 0, 2)).reshape(probe_count, block_total, panels)
    near_sum = lax.map(leaf_near, (jnp.moveaxis(positions, 1, 0), panel_areas, jnp.moveaxis(scaled, 1, 0)))
    near_sum = jnp.moveaxis(near_sum, 0, 1)
    offdiag_sketch = (full_sketch.astype(jnp.float32) - near_sum).astype(jnp.bfloat16)
    sort_index = jnp.broadcast_to(tree_order[None].astype(jnp.int32), offdiag_sketch.shape)
    sorted_off = jnp.take_along_axis(offdiag_sketch, sort_index, axis=3)
    sorted_probe = jnp.take_along_axis(probe_cols, sort_index, axis=3)

    def compress(items):
        off_leaf, probe_leaf, basis_leaf = items
        basis_flat = basis_leaf.reshape(-1, basis_leaf.shape[2])
        first = jnp.dot(off_leaf.reshape(probe_count, -1), basis_flat, preferred_element_type=jnp.float32)
        second = jnp.dot(probe_leaf.reshape(probe_count, -1), basis_flat, preferred_element_type=jnp.float32)
        return (first, second)
    sketch, probes = lax.map(compress, (jnp.moveaxis(sorted_off, 1, 0), jnp.moveaxis(sorted_probe, 1, 0), leaf_basis))
    for tree_level in range(transfer_mats.shape[1]):
        level_mats = transfer_mats[:, tree_level].astype(jnp.float32)
        partner = jnp.arange(node_count, dtype=jnp.int32) ^ 1 << tree_level
        sketch_proj = jnp.einsum('nrq,nqk->nrk', sketch, level_mats, precision=lax.Precision.HIGHEST)
        probe_proj = jnp.einsum('nrq,nqk->nrk', probes, level_mats, precision=lax.Precision.HIGHEST)
        sketch = sketch_proj + sketch_proj[partner]
        probes = probe_proj + probe_proj[partner]
    return (offdiag_sketch, jnp.stack([sketch, probes], axis=1))
```

```python
import math

import jax
import jax.numpy as jnp
from jax import lax
from jax.sharding import PartitionSpec as P

inv_four_pi = 1.0 / (4.0 * math.pi)


def partner(value, axis, bit):
    mask = 2**bit
    pairs = [(source, source ^ mask) for source in range(lax.axis_size(axis))]
    return lax.ppermute(value, axis, pairs)


def kernel_tile(target_pos, target_area, source_pos, source_area):
    distance = jnp.zeros((target_pos.shape[1], source_pos.shape[1]), jnp.float32)
    for component in range(3):
        gap = target_pos[component][:, None] - source_pos[component][None, :]
        distance = distance + gap * gap
    soft = distance + 0.5 * (target_area[:, None] + source_area[None, :])
    return (inv_four_pi * lax.rsqrt(soft)).astype(jnp.bfloat16)


def target_blocks(target_pos, target_area):
    panels = target_pos.shape[1]
    block_size = min(512, panels)
    block_count = panels // block_size
    pos_blocks = jnp.transpose(target_pos.reshape(3, block_count, block_size), (1, 0, 2))
    return (pos_blocks, target_area.reshape(block_count, block_size))


def near_block(target_pos, target_area, source_pos, source_area, source_scaled):
    pos_blocks, area_blocks = target_blocks(target_pos, target_area)

    def one_block(entry):
        block_pos, block_area = entry
        kernel = kernel_tile(block_pos, block_area, source_pos, source_area)
        return lax.dot_general(
            source_scaled, kernel, (((1,), (1,)), ((), ())), preferred_element_type=jnp.float32
        )

    sums = lax.map(one_block, (pos_blocks, area_blocks))
    return jnp.transpose(sums, (1, 0, 2)).reshape(source_scaled.shape[0], target_pos.shape[1])


def project(current, level_mat):
    return jnp.dot(current, level_mat.astype(jnp.float32), precision=lax.Precision.HIGHEST)


def climb_rows(rows, level_mats):
    for tree_level in range(level_mats.shape[0]):
        projected = project(rows, level_mats[tree_level])
        rows = projected + partner(projected, "leaf", tree_level)
    return rows


def shards(positions, panel_areas, probe_cols, full_sketch, tree_order, leaf_basis, transfer_mats):
    panels = positions.shape[3]
    probe_count = probe_cols.shape[0]
    basis_width = leaf_basis.shape[3]
    level_count = transfer_mats.shape[1]
    coords = positions.reshape(3, panels)
    area_row = panel_areas.reshape(1, panels)
    probe_flat = probe_cols.reshape(probe_count, panels)
    scaled = (area_row * probe_flat.astype(jnp.float32)).astype(jnp.bfloat16)
    sorting = tree_order.reshape(panels)
    basis_flat = leaf_basis.reshape(panels, basis_width)
    level_mats = transfer_mats.reshape(level_count, basis_width, basis_width)
    probe_part = jnp.dot(
        jnp.take(probe_flat, sorting, axis=1), basis_flat, preferred_element_type=jnp.float32
    )
    outgoing = jnp.concatenate([coords, area_row, scaled.astype(jnp.float32)], axis=0)
    piece = lax.all_gather(outgoing, "blk", axis=1, tiled=True)
    near_sum = near_block(coords, area_row[0], piece[:3], piece[3], piece[4:].astype(jnp.bfloat16))
    offdiag = (full_sketch.reshape(probe_count, panels).astype(jnp.float32) - near_sum).astype(
        jnp.bfloat16
    )
    sketch_part = jnp.dot(
        jnp.take(offdiag, sorting, axis=1), basis_flat, preferred_element_type=jnp.float32
    )
    stacked = jnp.concatenate([sketch_part, probe_part], axis=0)
    mine = lax.psum_scatter(stacked, "blk", scatter_dimension=0, tiled=True)
    top = climb_rows(mine, level_mats)
    nested = lax.all_gather(top, "blk", axis=0, tiled=True).reshape(2, probe_count, basis_width)[None]
    return (offdiag.reshape(probe_count, 1, 1, panels), nested)


def solution(mesh):
    in_specs = (
        P(None, "leaf", "blk", None),
        P("leaf", "blk", None),
        P(None, "leaf", "blk", None),
        P(None, "leaf", "blk", None),
        P("leaf", "blk", None),
        P("leaf", "blk", None, None),
        P("leaf", None, None, None),
    )
    out_specs = (P(None, "leaf", "blk", None), P("leaf", None, None, None))
    return jax.shard_map(shards, mesh=mesh, in_specs=in_specs, out_specs=out_specs, check_vma=False)
```

```python
import math

import jax
import jax.numpy as jnp
from jax import lax
from jax.sharding import PartitionSpec as P

inv_four_pi = 1.0 / (4.0 * math.pi)


def partner(value, axis, bit):
    mask = 2**bit
    pairs = [(source, source ^ mask) for source in range(lax.axis_size(axis))]
    return lax.ppermute(value, axis, pairs)


def kernel_tile(target_pos, target_area, source_pos, source_area):
    distance = jnp.zeros((target_pos.shape[1], source_pos.shape[1]), jnp.float32)
    for component in range(3):
        gap = target_pos[component][:, None] - source_pos[component][None, :]
        distance = distance + gap * gap
    soft = distance + 0.5 * (target_area[:, None] + source_area[None, :])
    return (inv_four_pi * lax.rsqrt(soft)).astype(jnp.bfloat16)


def target_blocks(target_pos, target_area):
    panels = target_pos.shape[1]
    block_size = min(512, panels)
    block_count = panels // block_size
    pos_blocks = jnp.transpose(target_pos.reshape(3, block_count, block_size), (1, 0, 2))
    return (pos_blocks, target_area.reshape(block_count, block_size))


def near_block(target_pos, target_area, source_pos, source_area, source_scaled):
    pos_blocks, area_blocks = target_blocks(target_pos, target_area)

    def one_block(entry):
        block_pos, block_area = entry
        kernel = kernel_tile(block_pos, block_area, source_pos, source_area)
        return lax.dot_general(
            source_scaled, kernel, (((1,), (1,)), ((), ())), preferred_element_type=jnp.float32
        )

    sums = lax.map(one_block, (pos_blocks, area_blocks))
    return jnp.transpose(sums, (1, 0, 2)).reshape(source_scaled.shape[0], target_pos.shape[1])


def project(current, level_mat):
    return jnp.dot(current, level_mat.astype(jnp.float32), precision=lax.Precision.HIGHEST)


def climb_rows(rows, level_mats):
    for tree_level in range(level_mats.shape[0]):
        projected = project(rows, level_mats[tree_level])
        rows = projected + partner(projected, "leaf", tree_level)
    return rows


def shards(positions, panel_areas, probe_cols, full_sketch, tree_order, leaf_basis, transfer_mats):
    panels = positions.shape[3]
    probe_count = probe_cols.shape[0]
    basis_width = leaf_basis.shape[3]
    level_count = transfer_mats.shape[1]
    coords = positions.reshape(3, panels)
    area_row = panel_areas.reshape(1, panels)
    probe_flat = probe_cols.reshape(probe_count, panels)
    scaled = (area_row * probe_flat.astype(jnp.float32)).astype(jnp.bfloat16)
    sorting = tree_order.reshape(panels)
    basis_flat = leaf_basis.reshape(panels, basis_width)
    level_mats = transfer_mats.reshape(level_count, basis_width, basis_width)
    probe_part = jnp.dot(
        jnp.take(probe_flat, sorting, axis=1), basis_flat, preferred_element_type=jnp.float32
    )
    outgoing = jnp.concatenate([coords, area_row, scaled.astype(jnp.float32)], axis=0)
    piece = lax.all_gather(outgoing, "ylo", axis=1, tiled=True)
    piece = lax.all_gather(piece, "core", axis=1, tiled=True)
    near_sum = near_block(coords, area_row[0], piece[:3], piece[3], piece[4:].astype(jnp.bfloat16))
    offdiag = (full_sketch.reshape(probe_count, panels).astype(jnp.float32) - near_sum).astype(
        jnp.bfloat16
    )
    sketch_part = jnp.dot(
        jnp.take(offdiag, sorting, axis=1), basis_flat, preferred_element_type=jnp.float32
    )
    stacked = jnp.concatenate([sketch_part, probe_part], axis=0)
    mine = lax.psum_scatter(stacked, "core", scatter_dimension=0, tiled=True)
    mine = lax.psum_scatter(mine, "ylo", scatter_dimension=0, tiled=True)
    top = climb_rows(mine, level_mats)
    top = lax.all_gather(top, "ylo", axis=0, tiled=True)
    nested = lax.all_gather(top, "core", axis=0, tiled=True).reshape(2, probe_count, basis_width)[None]
    return (offdiag.reshape(probe_count, 1, 1, panels), nested)


def solution(mesh):
    blk = mesh.shape["blk"]
    devices = mesh.devices.reshape(blk // 2, 2, mesh.shape["leaf"])
    split_mesh = jax.sharding.Mesh(devices, ("ylo", "core", "leaf"))
    blk_axes = ("ylo", "core")
    in_specs = (
        P(None, "leaf", blk_axes, None),
        P("leaf", blk_axes, None),
        P(None, "leaf", blk_axes, None),
        P(None, "leaf", blk_axes, None),
        P("leaf", blk_axes, None),
        P("leaf", blk_axes, None, None),
        P("leaf", None, None, None),
    )
    out_specs = (P(None, "leaf", blk_axes, None), P("leaf", None, None, None))
    return jax.shard_map(
        shards, mesh=split_mesh, in_specs=in_specs, out_specs=out_specs, check_vma=False
    )
```

```python
import math

import jax
import jax.numpy as jnp
from jax import lax
from jax.sharding import PartitionSpec as P

inv_four_pi = 1.0 / (4.0 * math.pi)


def partner(value, axis, bit):
    mask = 2**bit
    pairs = [(source, source ^ mask) for source in range(lax.axis_size(axis))]
    return lax.ppermute(value, axis, pairs)


def kernel_tile(target_pos, target_area, source_pos, source_area):
    distance = jnp.zeros((target_pos.shape[1], source_pos.shape[1]), jnp.float32)
    for component in range(3):
        gap = target_pos[component][:, None] - source_pos[component][None, :]
        distance = distance + gap * gap
    soft = distance + 0.5 * (target_area[:, None] + source_area[None, :])
    return (inv_four_pi * lax.rsqrt(soft)).astype(jnp.bfloat16)


def target_blocks(target_pos, target_area):
    panels = target_pos.shape[1]
    block_size = min(512, panels)
    block_count = panels // block_size
    pos_blocks = jnp.transpose(target_pos.reshape(3, block_count, block_size), (1, 0, 2))
    return (pos_blocks, target_area.reshape(block_count, block_size))


def near_block(target_pos, target_area, source_pos, source_area, source_scaled):
    pos_blocks, area_blocks = target_blocks(target_pos, target_area)

    def one_block(entry):
        block_pos, block_area = entry
        kernel = kernel_tile(block_pos, block_area, source_pos, source_area)
        return lax.dot_general(
            source_scaled, kernel, (((1,), (1,)), ((), ())), preferred_element_type=jnp.float32
        )

    sums = lax.map(one_block, (pos_blocks, area_blocks))
    return jnp.transpose(sums, (1, 0, 2)).reshape(source_scaled.shape[0], target_pos.shape[1])


def project(current, level_mat):
    return jnp.dot(current, level_mat.astype(jnp.float32), precision=lax.Precision.HIGHEST)


def climb_rows(rows, level_mats):
    for tree_level in range(level_mats.shape[0]):
        projected = project(rows, level_mats[tree_level])
        rows = projected + partner(projected, "leaf", tree_level)
    return rows


def swap_cores(value):
    return lax.ppermute(value, "core", [(0, 1), (1, 0)])


def shift_chips(value, step):
    count = lax.axis_size("ylo")
    return lax.ppermute(value, "ylo", [(source, (source + step) % count) for source in range(count)])


def gather_any_order(block, axis):
    count = lax.axis_size("ylo")
    parts = [block] + [shift_chips(block, step) for step in range(1, count)]
    chip_rows = jnp.concatenate(parts, axis)
    return jnp.concatenate([chip_rows, swap_cores(chip_rows)], axis)


def scatter_rows(value):
    count = lax.axis_size("ylo")
    chip = lax.axis_index("ylo")
    core = lax.axis_index("core")
    half = value.shape[0] // 2
    chunk = half // count
    width = value.shape[1]
    own_half = lax.dynamic_slice(value, (core * half, 0), (half, width))
    other_half = lax.dynamic_slice(value, ((1 - core) * half, 0), (half, width))
    summed = own_half + swap_cores(other_half)
    total = lax.dynamic_slice(summed, (chip * chunk, 0), (chunk, width))
    for step in range(1, count):
        target = (chip + step) % count
        outgoing = lax.dynamic_slice(summed, (target * chunk, 0), (chunk, width))
        total = total + shift_chips(outgoing, step)
    return total


def gather_rows(rows):
    count = lax.axis_size("ylo")
    chip = lax.axis_index("ylo")
    core = lax.axis_index("core")
    chunk, width = rows.shape
    half = jnp.zeros((count * chunk, width), rows.dtype)
    half = lax.dynamic_update_slice(half, rows, (chip * chunk, 0))
    for step in range(1, count):
        source = (chip + count - step) % count
        half = lax.dynamic_update_slice(half, shift_chips(rows, step), (source * chunk, 0))
    whole = jnp.zeros((2 * count * chunk, width), rows.dtype)
    whole = lax.dynamic_update_slice(whole, half, (core * count * chunk, 0))
    return lax.dynamic_update_slice(whole, swap_cores(half), ((1 - core) * count * chunk, 0))


def shards(positions, panel_areas, probe_cols, full_sketch, tree_order, leaf_basis, transfer_mats):
    panels = positions.shape[3]
    probe_count = probe_cols.shape[0]
    basis_width = leaf_basis.shape[3]
    level_count = transfer_mats.shape[1]
    coords = positions.reshape(3, panels)
    area_row = panel_areas.reshape(1, panels)
    probe_flat = probe_cols.reshape(probe_count, panels)
    scaled = (area_row * probe_flat.astype(jnp.float32)).astype(jnp.bfloat16)
    sorting = tree_order.reshape(panels)
    basis_flat = leaf_basis.reshape(panels, basis_width)
    level_mats = transfer_mats.reshape(level_count, basis_width, basis_width)
    probe_part = jnp.dot(
        jnp.take(probe_flat, sorting, axis=1), basis_flat, preferred_element_type=jnp.float32
    )
    outgoing = jnp.concatenate([coords, area_row, scaled.astype(jnp.float32)], axis=0)
    piece = gather_any_order(outgoing, 1)
    near_sum = near_block(coords, area_row[0], piece[:3], piece[3], piece[4:].astype(jnp.bfloat16))
    offdiag = (full_sketch.reshape(probe_count, panels).astype(jnp.float32) - near_sum).astype(
        jnp.bfloat16
    )
    sketch_part = jnp.dot(
        jnp.take(offdiag, sorting, axis=1), basis_flat, preferred_element_type=jnp.float32
    )
    stacked = jnp.concatenate([sketch_part, probe_part], axis=0)
    mine = scatter_rows(stacked)
    top = climb_rows(mine, level_mats)
    nested = gather_rows(top).reshape(2, probe_count, basis_width)[None]
    return (offdiag.reshape(probe_count, 1, 1, panels), nested)


def solution(mesh):
    blk = mesh.shape["blk"]
    devices = mesh.devices.reshape(blk // 2, 2, mesh.shape["leaf"])
    split_mesh = jax.sharding.Mesh(devices, ("ylo", "core", "leaf"))
    blk_axes = ("ylo", "core")
    in_specs = (
        P(None, "leaf", blk_axes, None),
        P("leaf", blk_axes, None),
        P(None, "leaf", blk_axes, None),
        P(None, "leaf", blk_axes, None),
        P("leaf", blk_axes, None),
        P("leaf", blk_axes, None, None),
        P("leaf", None, None, None),
    )
    out_specs = (P(None, "leaf", blk_axes, None), P("leaf", None, None, None))
    return jax.shard_map(
        shards, mesh=split_mesh, in_specs=in_specs, out_specs=out_specs, check_vma=False
    )
```

```python
import math

import jax
import jax.numpy as jnp
from jax import lax
from jax.sharding import PartitionSpec as P

inv_four_pi = 1.0 / (4.0 * math.pi)


def partner(value, axis, bit):
    mask = 2**bit
    pairs = [(source, source ^ mask) for source in range(lax.axis_size(axis))]
    return lax.ppermute(value, axis, pairs)


def kernel_tile(target_pos, target_area, source_pos, source_area):
    distance = jnp.zeros((target_pos.shape[1], source_pos.shape[1]), jnp.float32)
    for component in range(3):
        gap = target_pos[component][:, None] - source_pos[component][None, :]
        distance = distance + gap * gap
    soft = distance + 0.5 * (target_area[:, None] + source_area[None, :])
    return (inv_four_pi * lax.rsqrt(soft)).astype(jnp.bfloat16)


def target_blocks(target_pos, target_area):
    panels = target_pos.shape[1]
    block_size = min(512, panels)
    block_count = panels // block_size
    pos_blocks = jnp.transpose(target_pos.reshape(3, block_count, block_size), (1, 0, 2))
    return (pos_blocks, target_area.reshape(block_count, block_size))


def near_block(target_pos, target_area, source_pos, source_area, source_scaled):
    pos_blocks, area_blocks = target_blocks(target_pos, target_area)

    def one_block(entry):
        block_pos, block_area = entry
        kernel = kernel_tile(block_pos, block_area, source_pos, source_area)
        return lax.dot_general(
            source_scaled, kernel, (((1,), (1,)), ((), ())), preferred_element_type=jnp.float32
        )

    sums = lax.map(one_block, (pos_blocks, area_blocks))
    return jnp.transpose(sums, (1, 0, 2)).reshape(source_scaled.shape[0], target_pos.shape[1])


def project(current, level_mat):
    return jnp.dot(current, level_mat.astype(jnp.float32), precision=lax.Precision.HIGHEST)


def climb_rows(rows, level_mats):
    for tree_level in range(level_mats.shape[0]):
        projected = project(rows, level_mats[tree_level])
        rows = projected + partner(projected, "leaf", tree_level)
    return rows


def swap_cores(value):
    return lax.ppermute(value, "core", [(0, 1), (1, 0)])


def shift_chips(value, step):
    count = lax.axis_size("ylo")
    return lax.ppermute(value, "ylo", [(source, (source + step) % count) for source in range(count)])


def gather_any_order(block, axis):
    count = lax.axis_size("ylo")
    parts = [block] + [shift_chips(block, step) for step in range(1, count)]
    chip_rows = jnp.concatenate(parts, axis)
    return jnp.concatenate([chip_rows, swap_cores(chip_rows)], axis)


def scatter_rows(value):
    count = lax.axis_size("ylo")
    chip = lax.axis_index("ylo")
    core = lax.axis_index("core")
    half = value.shape[0] // 2
    chunk = half // count
    width = value.shape[1]
    own_half = lax.dynamic_slice(value, (core * half, 0), (half, width))
    other_half = lax.dynamic_slice(value, ((1 - core) * half, 0), (half, width))
    summed = own_half + swap_cores(other_half)
    total = lax.dynamic_slice(summed, (chip * chunk, 0), (chunk, width))
    for step in range(1, count):
        target = (chip + step) % count
        outgoing = lax.dynamic_slice(summed, (target * chunk, 0), (chunk, width))
        total = total + shift_chips(outgoing, step)
    return total


def gather_rows(rows):
    count = lax.axis_size("ylo")
    chip = lax.axis_index("ylo")
    core = lax.axis_index("core")
    chunk, width = rows.shape
    half = jnp.zeros((count * chunk, width), rows.dtype)
    half = lax.dynamic_update_slice(half, rows, (chip * chunk, 0))
    for step in range(1, count):
        source = (chip + count - step) % count
        half = lax.dynamic_update_slice(half, shift_chips(rows, step), (source * chunk, 0))
    whole = jnp.zeros((2 * count * chunk, width), rows.dtype)
    whole = lax.dynamic_update_slice(whole, half, (core * count * chunk, 0))
    return lax.dynamic_update_slice(whole, swap_cores(half), ((1 - core) * count * chunk, 0))


def shards(positions, panel_areas, probe_cols, full_sketch, tree_order, leaf_basis, transfer_mats):
    panels = positions.shape[3]
    probe_count = probe_cols.shape[0]
    basis_width = leaf_basis.shape[3]
    level_count = transfer_mats.shape[1]
    coords = positions.reshape(3, panels)
    area_row = panel_areas.reshape(1, panels)
    probe_flat = probe_cols.reshape(probe_count, panels)
    scaled = (area_row * probe_flat.astype(jnp.float32)).astype(jnp.bfloat16)
    sorting = tree_order.reshape(panels)
    basis_flat = leaf_basis.reshape(panels, basis_width)
    level_mats = transfer_mats.reshape(level_count, basis_width, basis_width)
    probe_part = jnp.dot(
        jnp.take(probe_flat, sorting, axis=1), basis_flat, preferred_element_type=jnp.float32
    )
    outgoing = jnp.concatenate([coords, area_row, scaled.astype(jnp.float32)], axis=0)
    piece = gather_any_order(outgoing, 1)
    near_sum = near_block(coords, area_row[0], piece[:3], piece[3], piece[4:].astype(jnp.bfloat16))
    offdiag = (full_sketch.reshape(probe_count, panels).astype(jnp.float32) - near_sum).astype(
        jnp.bfloat16
    )
    sketch_part = jnp.dot(
        jnp.take(offdiag, sorting, axis=1), basis_flat, preferred_element_type=jnp.float32
    )
    probe_top = gather_rows(climb_rows(scatter_rows(probe_part), level_mats))
    sketch_top = gather_rows(climb_rows(scatter_rows(sketch_part), level_mats))
    nested = jnp.stack([sketch_top, probe_top], axis=0)[None]
    return (offdiag.reshape(probe_count, 1, 1, panels), nested)


def solution(mesh):
    blk = mesh.shape["blk"]
    devices = mesh.devices.reshape(blk // 2, 2, mesh.shape["leaf"])
    split_mesh = jax.sharding.Mesh(devices, ("ylo", "core", "leaf"))
    blk_axes = ("ylo", "core")
    in_specs = (
        P(None, "leaf", blk_axes, None),
        P("leaf", blk_axes, None),
        P(None, "leaf", blk_axes, None),
        P(None, "leaf", blk_axes, None),
        P("leaf", blk_axes, None),
        P("leaf", blk_axes, None, None),
        P("leaf", None, None, None),
    )
    out_specs = (P(None, "leaf", blk_axes, None), P("leaf", None, None, None))
    return jax.shard_map(
        shards, mesh=split_mesh, in_specs=in_specs, out_specs=out_specs, check_vma=False
    )
```

```python
import math

import jax
import jax.numpy as jnp
from jax import lax
from jax.sharding import PartitionSpec as P

inv_four_pi = 1.0 / (4.0 * math.pi)


def partner(value, axis, bit):
    mask = 2**bit
    pairs = [(source, source ^ mask) for source in range(lax.axis_size(axis))]
    return lax.ppermute(value, axis, pairs)


def kernel_tile(target_pos, target_area, source_pos, source_area):
    distance = jnp.zeros((target_pos.shape[1], source_pos.shape[1]), jnp.float32)
    for component in range(3):
        gap = target_pos[component][:, None] - source_pos[component][None, :]
        distance = distance + gap * gap
    soft = distance + 0.5 * (target_area[:, None] + source_area[None, :])
    return (inv_four_pi * lax.rsqrt(soft)).astype(jnp.bfloat16)


def target_blocks(target_pos, target_area):
    panels = target_pos.shape[1]
    block_size = min(512, panels)
    block_count = panels // block_size
    pos_blocks = jnp.transpose(target_pos.reshape(3, block_count, block_size), (1, 0, 2))
    return (pos_blocks, target_area.reshape(block_count, block_size))


def near_block(target_pos, target_area, source_pos, source_area, source_scaled):
    pos_blocks, area_blocks = target_blocks(target_pos, target_area)

    def one_block(entry):
        block_pos, block_area = entry
        kernel = kernel_tile(block_pos, block_area, source_pos, source_area)
        return lax.dot_general(
            source_scaled, kernel, (((1,), (1,)), ((), ())), preferred_element_type=jnp.float32
        )

    sums = lax.map(one_block, (pos_blocks, area_blocks))
    return jnp.transpose(sums, (1, 0, 2)).reshape(source_scaled.shape[0], target_pos.shape[1])


def project(current, level_mat):
    return jnp.dot(current, level_mat.astype(jnp.float32), precision=lax.Precision.HIGHEST)


def climb_rows(rows, level_mats):
    for tree_level in range(level_mats.shape[0]):
        projected = project(rows, level_mats[tree_level])
        rows = projected + partner(projected, "leaf", tree_level)
    return rows


def exchange(value, axis):
    return lax.all_to_all(value, axis, 0, 0, tiled=True)


def gather_blocks(block, axis):
    count = lax.axis_size(axis)
    return exchange(jnp.concatenate([block] * count, axis=0), axis)


def scatter_rows(value):
    width = value.shape[1]
    halves = exchange(value, "core").reshape(2, -1, width)
    summed = halves[0] + halves[1]
    count = lax.axis_size("ylo")
    return exchange(summed, "ylo").reshape(count, -1, width).sum(axis=0)


def gather_rows(rows):
    return gather_blocks(gather_blocks(rows, "ylo"), "core")


def shards(positions, panel_areas, probe_cols, full_sketch, tree_order, leaf_basis, transfer_mats):
    panels = positions.shape[3]
    probe_count = probe_cols.shape[0]
    basis_width = leaf_basis.shape[3]
    level_count = transfer_mats.shape[1]
    coords = positions.reshape(3, panels)
    area_row = panel_areas.reshape(1, panels)
    probe_flat = probe_cols.reshape(probe_count, panels)
    scaled = (area_row * probe_flat.astype(jnp.float32)).astype(jnp.bfloat16)
    sorting = tree_order.reshape(panels)
    basis_flat = leaf_basis.reshape(panels, basis_width)
    level_mats = transfer_mats.reshape(level_count, basis_width, basis_width)
    probe_part = jnp.dot(
        jnp.take(probe_flat, sorting, axis=1), basis_flat, preferred_element_type=jnp.float32
    )
    outgoing = jnp.concatenate([coords, area_row, scaled.astype(jnp.float32)], axis=0)
    rows_out = outgoing.shape[0]
    stacked_blocks = gather_blocks(gather_blocks(outgoing, "ylo"), "core")
    piece = jnp.transpose(stacked_blocks.reshape(-1, rows_out, panels), (1, 0, 2)).reshape(rows_out, -1)
    near_sum = near_block(coords, area_row[0], piece[:3], piece[3], piece[4:].astype(jnp.bfloat16))
    offdiag = (full_sketch.reshape(probe_count, panels).astype(jnp.float32) - near_sum).astype(
        jnp.bfloat16
    )
    sketch_part = jnp.dot(
        jnp.take(offdiag, sorting, axis=1), basis_flat, preferred_element_type=jnp.float32
    )
    stacked = jnp.concatenate([sketch_part, probe_part], axis=0)
    mine = scatter_rows(stacked)
    top = climb_rows(mine, level_mats)
    nested = gather_rows(top).reshape(2, probe_count, basis_width)[None]
    return (offdiag.reshape(probe_count, 1, 1, panels), nested)


def solution(mesh):
    blk = mesh.shape["blk"]
    devices = mesh.devices.reshape(blk // 2, 2, mesh.shape["leaf"])
    split_mesh = jax.sharding.Mesh(devices, ("ylo", "core", "leaf"))
    blk_axes = ("ylo", "core")
    in_specs = (
        P(None, "leaf", blk_axes, None),
        P("leaf", blk_axes, None),
        P(None, "leaf", blk_axes, None),
        P(None, "leaf", blk_axes, None),
        P("leaf", blk_axes, None),
        P("leaf", blk_axes, None, None),
        P("leaf", None, None, None),
    )
    out_specs = (P(None, "leaf", blk_axes, None), P("leaf", None, None, None))
    return jax.shard_map(
        shards, mesh=split_mesh, in_specs=in_specs, out_specs=out_specs, check_vma=False
    )
```

```python
import math

import jax
import jax.numpy as jnp
from jax import lax
from jax.sharding import PartitionSpec as P

inv_four_pi = 1.0 / (4.0 * math.pi)


def partner(value, axis, bit):
    mask = 2**bit
    pairs = [(source, source ^ mask) for source in range(lax.axis_size(axis))]
    return lax.ppermute(value, axis, pairs)


def kernel_tile(target_pos, target_area, source_pos, source_area):
    distance = jnp.zeros((target_pos.shape[1], source_pos.shape[1]), jnp.float32)
    for component in range(3):
        gap = target_pos[component][:, None] - source_pos[component][None, :]
        distance = distance + gap * gap
    soft = distance + 0.5 * (target_area[:, None] + source_area[None, :])
    return (inv_four_pi * lax.rsqrt(soft)).astype(jnp.bfloat16)


def target_blocks(target_pos, target_area):
    panels = target_pos.shape[1]
    block_size = min(512, panels)
    block_count = panels // block_size
    pos_blocks = jnp.transpose(target_pos.reshape(3, block_count, block_size), (1, 0, 2))
    return (pos_blocks, target_area.reshape(block_count, block_size))


def near_block(target_pos, target_area, source_pos, source_area, source_scaled):
    pos_blocks, area_blocks = target_blocks(target_pos, target_area)

    def one_block(entry):
        block_pos, block_area = entry
        kernel = kernel_tile(block_pos, block_area, source_pos, source_area)
        return lax.dot_general(
            source_scaled, kernel, (((1,), (1,)), ((), ())), preferred_element_type=jnp.float32
        )

    sums = lax.map(one_block, (pos_blocks, area_blocks))
    return jnp.transpose(sums, (1, 0, 2)).reshape(source_scaled.shape[0], target_pos.shape[1])


def project(current, level_mat):
    return jnp.dot(current, level_mat.astype(jnp.float32), precision=lax.Precision.HIGHEST)


def climb_rows(rows, level_mats):
    for tree_level in range(level_mats.shape[0]):
        projected = project(rows, level_mats[tree_level])
        rows = projected + partner(projected, "leaf", tree_level)
    return rows


def exchange(value, axis):
    return lax.all_to_all(value, axis, 0, 0, tiled=True)


def gather_blocks(block, axis):
    count = lax.axis_size(axis)
    return exchange(jnp.concatenate([block] * count, axis=0), axis)


def scatter_rows(value):
    width = value.shape[1]
    halves = exchange(value, "core").reshape(2, -1, width)
    summed = halves[0] + halves[1]
    count = lax.axis_size("ylo")
    return exchange(summed, "ylo").reshape(count, -1, width).sum(axis=0)


def gather_rows(rows):
    return gather_blocks(gather_blocks(rows, "ylo"), "core")


def shards(positions, panel_areas, probe_cols, full_sketch, tree_order, leaf_basis, transfer_mats):
    panels = positions.shape[3]
    probe_count = probe_cols.shape[0]
    basis_width = leaf_basis.shape[3]
    level_count = transfer_mats.shape[1]
    coords = positions.reshape(3, panels)
    area_row = panel_areas.reshape(1, panels)
    probe_flat = probe_cols.reshape(probe_count, panels)
    sketch_flat = full_sketch.reshape(probe_count, panels)
    scaled = (area_row * probe_flat.astype(jnp.float32)).astype(jnp.bfloat16)
    sorting = tree_order.reshape(panels)
    basis_flat = leaf_basis.reshape(panels, basis_width)
    level_mats = transfer_mats.reshape(level_count, basis_width, basis_width)
    geometry = jnp.concatenate([coords, area_row], axis=0)
    geometry_rows = geometry.shape[0]
    chunk_count = 2
    chunk = probe_count // chunk_count
    offdiag_chunks, sketch_chunks, probe_chunks = [], [], []
    for index in range(chunk_count):
        rows = slice(index * chunk, (index + 1) * chunk)
        scaled_rows = scaled[rows].astype(jnp.float32)
        outgoing = jnp.concatenate([geometry, scaled_rows], axis=0)
        width_out = outgoing.shape[0]
        blocks = gather_rows(outgoing)
        piece = jnp.transpose(blocks.reshape(-1, width_out, panels), (1, 0, 2)).reshape(width_out, -1)
        source_geometry = piece[:geometry_rows]
        piece = piece[geometry_rows:]
        near_sum = near_block(
            coords, area_row[0], source_geometry[:3], source_geometry[3], piece.astype(jnp.bfloat16)
        )
        offdiag = (sketch_flat[rows].astype(jnp.float32) - near_sum).astype(jnp.bfloat16)
        sketch_part = jnp.dot(
            jnp.take(offdiag, sorting, axis=1), basis_flat, preferred_element_type=jnp.float32
        )
        probe_part = jnp.dot(
            jnp.take(probe_flat[rows], sorting, axis=1), basis_flat, preferred_element_type=jnp.float32
        )
        stacked = jnp.concatenate([sketch_part, probe_part], axis=0)
        top = gather_rows(climb_rows(scatter_rows(stacked), level_mats))
        offdiag_chunks.append(offdiag)
        sketch_chunks.append(top[:chunk])
        probe_chunks.append(top[chunk:])
    offdiag = jnp.concatenate(offdiag_chunks, axis=0)
    nested = jnp.stack(
        [jnp.concatenate(sketch_chunks, axis=0), jnp.concatenate(probe_chunks, axis=0)], axis=0
    )[None]
    return (offdiag.reshape(probe_count, 1, 1, panels), nested)


def solution(mesh):
    blk = mesh.shape["blk"]
    devices = mesh.devices.reshape(blk // 2, 2, mesh.shape["leaf"])
    split_mesh = jax.sharding.Mesh(devices, ("ylo", "core", "leaf"))
    blk_axes = ("ylo", "core")
    in_specs = (
        P(None, "leaf", blk_axes, None),
        P("leaf", blk_axes, None),
        P(None, "leaf", blk_axes, None),
        P(None, "leaf", blk_axes, None),
        P("leaf", blk_axes, None),
        P("leaf", blk_axes, None, None),
        P("leaf", None, None, None),
    )
    out_specs = (P(None, "leaf", blk_axes, None), P("leaf", None, None, None))
    return jax.shard_map(
        shards, mesh=split_mesh, in_specs=in_specs, out_specs=out_specs, check_vma=False
    )
```

```python
import math

import jax
import jax.numpy as jnp
from jax import lax
from jax.experimental import pallas as pl
from jax.sharding import PartitionSpec as P

inv_four_pi = 1.0 / (4.0 * math.pi)


def partner(value, axis, bit):
    mask = 2**bit
    pairs = [(source, source ^ mask) for source in range(lax.axis_size(axis))]
    return lax.ppermute(value, axis, pairs)


def kernel_tile(target_pos, target_area, source_pos, source_area):
    distance = jnp.zeros((target_pos.shape[1], source_pos.shape[1]), jnp.float32)
    for component in range(3):
        gap = target_pos[component][:, None] - source_pos[component][None, :]
        distance = distance + gap * gap
    soft = distance + 0.5 * (target_area[:, None] + source_area[None, :])
    return (inv_four_pi * lax.rsqrt(soft)).astype(jnp.bfloat16)


def target_blocks(target_pos, target_area):
    panels = target_pos.shape[1]
    block_size = min(512, panels)
    block_count = panels // block_size
    pos_blocks = jnp.transpose(target_pos.reshape(3, block_count, block_size), (1, 0, 2))
    return (pos_blocks, target_area.reshape(block_count, block_size))


def near_block(target_pos, target_area, source_pos, source_area, source_scaled):
    pos_blocks, area_blocks = target_blocks(target_pos, target_area)

    def one_block(entry):
        block_pos, block_area = entry
        kernel = kernel_tile(block_pos, block_area, source_pos, source_area)
        return lax.dot_general(
            source_scaled, kernel, (((1,), (1,)), ((), ())), preferred_element_type=jnp.float32
        )

    sums = lax.map(one_block, (pos_blocks, area_blocks))
    return jnp.transpose(sums, (1, 0, 2)).reshape(source_scaled.shape[0], target_pos.shape[1])


def project(current, level_mat):
    return jnp.dot(current, level_mat.astype(jnp.float32), precision=lax.Precision.HIGHEST)


def climb_rows(rows, level_mats):
    for tree_level in range(level_mats.shape[0]):
        projected = project(rows, level_mats[tree_level])
        rows = projected + partner(projected, "leaf", tree_level)
    return rows


def exchange(value, axis):
    return lax.all_to_all(value, axis, 0, 0, tiled=True)


def gather_blocks(block, axis):
    count = lax.axis_size(axis)
    return exchange(jnp.concatenate([block] * count, axis=0), axis)


def scatter_rows(value):
    width = value.shape[1]
    halves = exchange(value, "core").reshape(2, -1, width)
    summed = halves[0] + halves[1]
    count = lax.axis_size("ylo")
    return exchange(summed, "ylo").reshape(count, -1, width).sum(axis=0)


def gather_rows(rows):
    return gather_blocks(gather_blocks(rows, "ylo"), "core")


def near_project_kernel(target_ref, source_ref, sketch_ref, probe_ref, order_ref, basis_ref, off_ref, parts_ref):
    block_count = source_ref.shape[0]
    probe_count, panels = sketch_ref.shape
    geometry_rows = source_ref.shape[1] - probe_count
    target = target_ref[...]
    near = jnp.zeros((probe_count, panels), jnp.float32)
    for block in range(block_count):
        geometry = source_ref[block, 0:geometry_rows, :]
        distance = jnp.zeros((panels, panels), jnp.float32)
        for component in range(3):
            gap = target[:, component : component + 1] - geometry[component : component + 1, :]
            distance = distance + gap * gap
        soft = distance + 0.5 * (target[:, 3:4] + geometry[3:4, :])
        tile = (inv_four_pi * lax.rsqrt(soft)).astype(jnp.bfloat16)
        scaled = source_ref[block, geometry_rows:, :].astype(jnp.bfloat16)
        near = near + lax.dot_general(
            scaled, tile, (((1,), (1,)), ((), ())), preferred_element_type=jnp.float32
        )
    off = (sketch_ref[...].astype(jnp.float32) - near).astype(jnp.bfloat16)
    off_ref[...] = off
    lanes = lax.broadcasted_iota(jnp.int32, (panels, panels), 1)
    onehot = (order_ref[...] == lanes).astype(jnp.bfloat16)
    basis = basis_ref[...]
    for index, values in enumerate((off, probe_ref[...])):
        ordered = lax.dot_general(
            values, onehot, (((1,), (1,)), ((), ())), preferred_element_type=jnp.float32
        ).astype(jnp.bfloat16)
        parts_ref[index * probe_count : (index + 1) * probe_count, :] = jnp.dot(
            ordered, basis, preferred_element_type=jnp.float32
        )


def near_project(target, source, sketch, probe, order, basis):
    probe_count, panels = sketch.shape
    width = basis.shape[1]
    blocks = source.shape[0]
    flops = 2 * probe_count * panels * (blocks * panels + 2 * panels + 2 * width)
    bytes_accessed = 4 * source.size + 2 * (3 * sketch.size + basis.size) + 8 * probe_count * width
    return pl.pallas_call(
        near_project_kernel,
        out_shape=(
            jax.ShapeDtypeStruct((probe_count, panels), jnp.bfloat16),
            jax.ShapeDtypeStruct((2 * probe_count, width), jnp.float32),
        ),
        cost_estimate=pl.CostEstimate(
            flops=flops, transcendentals=blocks * panels * panels, bytes_accessed=bytes_accessed
        ),
    )(target, source, sketch, probe, order, basis)


def shards(positions, panel_areas, probe_cols, full_sketch, tree_order, leaf_basis, transfer_mats):
    panels = positions.shape[3]
    probe_count = probe_cols.shape[0]
    basis_width = leaf_basis.shape[3]
    level_count = transfer_mats.shape[1]
    coords = positions.reshape(3, panels)
    area_row = panel_areas.reshape(1, panels)
    probe_flat = probe_cols.reshape(probe_count, panels)
    scaled = (area_row * probe_flat.astype(jnp.float32)).astype(jnp.bfloat16)
    basis_flat = leaf_basis.reshape(panels, basis_width)
    level_mats = transfer_mats.reshape(level_count, basis_width, basis_width)
    geometry = jnp.concatenate([coords, area_row, jnp.zeros((4, panels), jnp.float32)], axis=0)
    outgoing = jnp.concatenate([geometry, scaled.astype(jnp.float32)], axis=0)
    blocks = gather_blocks(gather_blocks(outgoing, "ylo"), "core")
    source = blocks.reshape(-1, outgoing.shape[0], panels)
    offdiag, stacked = near_project(
        jnp.transpose(geometry),
        source,
        full_sketch.reshape(probe_count, panels),
        probe_flat,
        tree_order.reshape(panels, 1),
        basis_flat,
    )
    mine = scatter_rows(stacked)
    top = climb_rows(mine, level_mats)
    nested = gather_rows(top).reshape(2, probe_count, basis_width)[None]
    return (offdiag.reshape(probe_count, 1, 1, panels), nested)


def solution(mesh):
    blk = mesh.shape["blk"]
    devices = mesh.devices.reshape(blk // 2, 2, mesh.shape["leaf"])
    split_mesh = jax.sharding.Mesh(devices, ("ylo", "core", "leaf"))
    blk_axes = ("ylo", "core")
    in_specs = (
        P(None, "leaf", blk_axes, None),
        P("leaf", blk_axes, None),
        P(None, "leaf", blk_axes, None),
        P(None, "leaf", blk_axes, None),
        P("leaf", blk_axes, None),
        P("leaf", blk_axes, None, None),
        P("leaf", None, None, None),
    )
    out_specs = (P(None, "leaf", blk_axes, None), P("leaf", None, None, None))
    return jax.shard_map(
        shards, mesh=split_mesh, in_specs=in_specs, out_specs=out_specs, check_vma=False
    )
```

```python
import math

import jax
import jax.numpy as jnp
from jax import lax
from jax.experimental import pallas as pl
from jax.sharding import PartitionSpec as P

inv_four_pi = 1.0 / (4.0 * math.pi)


def partner(value, axis, bit):
    mask = 2**bit
    pairs = [(source, source ^ mask) for source in range(lax.axis_size(axis))]
    return lax.ppermute(value, axis, pairs)


def kernel_tile(target_pos, target_area, source_pos, source_area):
    distance = jnp.zeros((target_pos.shape[1], source_pos.shape[1]), jnp.float32)
    for component in range(3):
        gap = target_pos[component][:, None] - source_pos[component][None, :]
        distance = distance + gap * gap
    soft = distance + 0.5 * (target_area[:, None] + source_area[None, :])
    return (inv_four_pi * lax.rsqrt(soft)).astype(jnp.bfloat16)


def target_blocks(target_pos, target_area):
    panels = target_pos.shape[1]
    block_size = min(512, panels)
    block_count = panels // block_size
    pos_blocks = jnp.transpose(target_pos.reshape(3, block_count, block_size), (1, 0, 2))
    return (pos_blocks, target_area.reshape(block_count, block_size))


def near_block(target_pos, target_area, source_pos, source_area, source_scaled):
    pos_blocks, area_blocks = target_blocks(target_pos, target_area)

    def one_block(entry):
        block_pos, block_area = entry
        kernel = kernel_tile(block_pos, block_area, source_pos, source_area)
        return lax.dot_general(
            source_scaled, kernel, (((1,), (1,)), ((), ())), preferred_element_type=jnp.float32
        )

    sums = lax.map(one_block, (pos_blocks, area_blocks))
    return jnp.transpose(sums, (1, 0, 2)).reshape(source_scaled.shape[0], target_pos.shape[1])


def project(current, level_mat):
    return jnp.dot(current, level_mat.astype(jnp.float32), precision=lax.Precision.HIGHEST)


def climb_rows(rows, level_mats):
    for tree_level in range(level_mats.shape[0]):
        projected = project(rows, level_mats[tree_level])
        rows = projected + partner(projected, "leaf", tree_level)
    return rows


def exchange(value, axis):
    return lax.all_to_all(value, axis, 0, 0, tiled=True)


def gather_blocks(block, axis):
    count = lax.axis_size(axis)
    copies = jnp.broadcast_to(block[None], (count,) + block.shape)
    return exchange(copies.reshape((count * block.shape[0],) + block.shape[1:]), axis)


def scatter_rows(value):
    width = value.shape[1]
    halves = exchange(value, "core").reshape(2, -1, width)
    summed = halves[0] + halves[1]
    count = lax.axis_size("ylo")
    return exchange(summed, "ylo").reshape(count, -1, width).sum(axis=0)


def gather_rows(rows):
    return gather_blocks(gather_blocks(rows, "ylo"), "core")


def near_project_kernel(target_ref, source_ref, sketch_ref, probe_ref, order_ref, basis_ref, off_ref, parts_ref):
    block_count = source_ref.shape[0]
    probe_count, panels = sketch_ref.shape
    geometry_rows = source_ref.shape[1] - probe_count
    target = target_ref[...]
    near = jnp.zeros((probe_count, panels), jnp.float32)
    for block in range(block_count):
        geometry = source_ref[block, 0:geometry_rows, :]
        distance = jnp.zeros((panels, panels), jnp.float32)
        for component in range(3):
            gap = target[:, component : component + 1] - geometry[component : component + 1, :]
            distance = distance + gap * gap
        soft = distance + 0.5 * (target[:, 3:4] + geometry[3:4, :])
        tile = (inv_four_pi * lax.rsqrt(soft)).astype(jnp.bfloat16)
        scaled = source_ref[block, geometry_rows:, :].astype(jnp.bfloat16)
        near = near + lax.dot_general(
            scaled, tile, (((1,), (1,)), ((), ())), preferred_element_type=jnp.float32
        )
    off = (sketch_ref[...].astype(jnp.float32) - near).astype(jnp.bfloat16)
    off_ref[...] = off
    lanes = lax.broadcasted_iota(jnp.int32, (panels, panels), 1)
    onehot = (order_ref[...] == lanes).astype(jnp.bfloat16)
    basis = basis_ref[...]
    for index, values in enumerate((off, probe_ref[...])):
        ordered = lax.dot_general(
            values, onehot, (((1,), (1,)), ((), ())), preferred_element_type=jnp.float32
        ).astype(jnp.bfloat16)
        parts_ref[index * probe_count : (index + 1) * probe_count, :] = jnp.dot(
            ordered, basis, preferred_element_type=jnp.float32
        )


def near_project(target, source, sketch, probe, order, basis):
    probe_count, panels = sketch.shape
    width = basis.shape[1]
    blocks = source.shape[0]
    flops = 2 * probe_count * panels * (blocks * panels + 2 * panels + 2 * width)
    bytes_accessed = 4 * source.size + 2 * (3 * sketch.size + basis.size) + 8 * probe_count * width
    return pl.pallas_call(
        near_project_kernel,
        out_shape=(
            jax.ShapeDtypeStruct((probe_count, panels), jnp.bfloat16),
            jax.ShapeDtypeStruct((2 * probe_count, width), jnp.float32),
        ),
        cost_estimate=pl.CostEstimate(
            flops=flops, transcendentals=blocks * panels * panels, bytes_accessed=bytes_accessed
        ),
    )(target, source, sketch, probe, order, basis)


def shards(positions, panel_areas, probe_cols, full_sketch, tree_order, leaf_basis, transfer_mats):
    panels = positions.shape[3]
    probe_count = probe_cols.shape[0]
    basis_width = leaf_basis.shape[3]
    level_count = transfer_mats.shape[1]
    coords = positions.reshape(3, panels)
    area_row = panel_areas.reshape(1, panels)
    probe_flat = probe_cols.reshape(probe_count, panels)
    scaled = (area_row * probe_flat.astype(jnp.float32)).astype(jnp.bfloat16)
    basis_flat = leaf_basis.reshape(panels, basis_width)
    level_mats = transfer_mats.reshape(level_count, basis_width, basis_width)
    geometry = jnp.concatenate([coords, area_row, jnp.zeros((4, panels), jnp.float32)], axis=0)
    outgoing = jnp.concatenate([geometry, scaled.astype(jnp.float32)], axis=0)
    blocks = gather_blocks(gather_blocks(outgoing, "ylo"), "core")
    source = blocks.reshape(-1, outgoing.shape[0], panels)
    offdiag, stacked = near_project(
        jnp.transpose(geometry),
        source,
        full_sketch.reshape(probe_count, panels),
        probe_flat,
        tree_order.reshape(panels, 1),
        basis_flat,
    )
    mine = scatter_rows(stacked)
    top = climb_rows(mine, level_mats)
    nested = gather_rows(top).reshape(2, probe_count, basis_width)[None]
    return (offdiag.reshape(probe_count, 1, 1, panels), nested)


def solution(mesh):
    blk = mesh.shape["blk"]
    devices = mesh.devices.reshape(blk // 2, 2, mesh.shape["leaf"])
    split_mesh = jax.sharding.Mesh(devices, ("ylo", "core", "leaf"))
    blk_axes = ("ylo", "core")
    in_specs = (
        P(None, "leaf", blk_axes, None),
        P("leaf", blk_axes, None),
        P(None, "leaf", blk_axes, None),
        P(None, "leaf", blk_axes, None),
        P("leaf", blk_axes, None),
        P("leaf", blk_axes, None, None),
        P("leaf", None, None, None),
    )
    out_specs = (P(None, "leaf", blk_axes, None), P("leaf", None, None, None))
    return jax.shard_map(
        shards, mesh=split_mesh, in_specs=in_specs, out_specs=out_specs, check_vma=False
    )
```

```python
import math

import jax
import jax.numpy as jnp
from jax import lax
from jax.experimental import pallas as pl
from jax.sharding import PartitionSpec as P

inv_four_pi = 1.0 / (4.0 * math.pi)


def partner(value, axis, bit):
    mask = 2**bit
    pairs = [(source, source ^ mask) for source in range(lax.axis_size(axis))]
    return lax.ppermute(value, axis, pairs)


def kernel_tile(target_pos, target_area, source_pos, source_area):
    distance = jnp.zeros((target_pos.shape[1], source_pos.shape[1]), jnp.float32)
    for component in range(3):
        gap = target_pos[component][:, None] - source_pos[component][None, :]
        distance = distance + gap * gap
    soft = distance + 0.5 * (target_area[:, None] + source_area[None, :])
    return (inv_four_pi * lax.rsqrt(soft)).astype(jnp.bfloat16)


def target_blocks(target_pos, target_area):
    panels = target_pos.shape[1]
    block_size = min(512, panels)
    block_count = panels // block_size
    pos_blocks = jnp.transpose(target_pos.reshape(3, block_count, block_size), (1, 0, 2))
    return (pos_blocks, target_area.reshape(block_count, block_size))


def near_block(target_pos, target_area, source_pos, source_area, source_scaled):
    pos_blocks, area_blocks = target_blocks(target_pos, target_area)

    def one_block(entry):
        block_pos, block_area = entry
        kernel = kernel_tile(block_pos, block_area, source_pos, source_area)
        return lax.dot_general(
            source_scaled, kernel, (((1,), (1,)), ((), ())), preferred_element_type=jnp.float32
        )

    sums = lax.map(one_block, (pos_blocks, area_blocks))
    return jnp.transpose(sums, (1, 0, 2)).reshape(source_scaled.shape[0], target_pos.shape[1])


def project(current, level_mat):
    return jnp.dot(current, level_mat.astype(jnp.float32), precision=lax.Precision.HIGHEST)


LEVEL_AXES = ("lx0", "lx1", "lyhi")


def climb_rows(rows, level_mats):
    for tree_level in range(level_mats.shape[0]):
        projected = project(rows, level_mats[tree_level])
        pair = gather_blocks(projected, LEVEL_AXES[tree_level])
        rows = pair[: projected.shape[0]] + pair[projected.shape[0] :]
    return rows


def exchange(value, axis):
    return lax.all_to_all(value, axis, 0, 0, tiled=True)


def gather_blocks(block, axis):
    count = lax.axis_size(axis)
    copies = jnp.broadcast_to(block[None], (count,) + block.shape)
    return exchange(copies.reshape((count * block.shape[0],) + block.shape[1:]), axis)


def scatter_rows(value):
    width = value.shape[1]
    halves = exchange(value, "core").reshape(2, -1, width)
    summed = halves[0] + halves[1]
    count = lax.axis_size("ylo")
    return exchange(summed, "ylo").reshape(count, -1, width).sum(axis=0)


def gather_rows(rows):
    return gather_blocks(gather_blocks(rows, "ylo"), "core")


def near_project_kernel(target_ref, source_ref, sketch_ref, probe_ref, order_ref, basis_ref, off_ref, parts_ref):
    block_count = source_ref.shape[0]
    probe_count, panels = sketch_ref.shape
    geometry_rows = source_ref.shape[1] - probe_count
    target = target_ref[...]
    near = jnp.zeros((probe_count, panels), jnp.float32)
    for block in range(block_count):
        geometry = source_ref[block, 0:geometry_rows, :]
        distance = jnp.zeros((panels, panels), jnp.float32)
        for component in range(3):
            gap = target[:, component : component + 1] - geometry[component : component + 1, :]
            distance = distance + gap * gap
        soft = distance + 0.5 * (target[:, 3:4] + geometry[3:4, :])
        tile = (inv_four_pi * lax.rsqrt(soft)).astype(jnp.bfloat16)
        scaled = source_ref[block, geometry_rows:, :].astype(jnp.bfloat16)
        near = near + lax.dot_general(
            scaled, tile, (((1,), (1,)), ((), ())), preferred_element_type=jnp.float32
        )
    off = (sketch_ref[...].astype(jnp.float32) - near).astype(jnp.bfloat16)
    off_ref[...] = off
    lanes = lax.broadcasted_iota(jnp.int32, (panels, panels), 1)
    onehot = (order_ref[...] == lanes).astype(jnp.bfloat16)
    basis = basis_ref[...]
    for index, values in enumerate((off, probe_ref[...])):
        ordered = lax.dot_general(
            values, onehot, (((1,), (1,)), ((), ())), preferred_element_type=jnp.float32
        ).astype(jnp.bfloat16)
        parts_ref[index * probe_count : (index + 1) * probe_count, :] = jnp.dot(
            ordered, basis, preferred_element_type=jnp.float32
        )


def near_project(target, source, sketch, probe, order, basis):
    probe_count, panels = sketch.shape
    width = basis.shape[1]
    blocks = source.shape[0]
    flops = 2 * probe_count * panels * (blocks * panels + 2 * panels + 2 * width)
    bytes_accessed = 4 * source.size + 2 * (3 * sketch.size + basis.size) + 8 * probe_count * width
    return pl.pallas_call(
        near_project_kernel,
        out_shape=(
            jax.ShapeDtypeStruct((probe_count, panels), jnp.bfloat16),
            jax.ShapeDtypeStruct((2 * probe_count, width), jnp.float32),
        ),
        cost_estimate=pl.CostEstimate(
            flops=flops, transcendentals=blocks * panels * panels, bytes_accessed=bytes_accessed
        ),
    )(target, source, sketch, probe, order, basis)


def shards(positions, panel_areas, probe_cols, full_sketch, tree_order, leaf_basis, transfer_mats):
    panels = positions.shape[3]
    probe_count = probe_cols.shape[0]
    basis_width = leaf_basis.shape[3]
    level_count = transfer_mats.shape[1]
    coords = positions.reshape(3, panels)
    area_row = panel_areas.reshape(1, panels)
    probe_flat = probe_cols.reshape(probe_count, panels)
    scaled = (area_row * probe_flat.astype(jnp.float32)).astype(jnp.bfloat16)
    basis_flat = leaf_basis.reshape(panels, basis_width)
    level_mats = transfer_mats.reshape(level_count, basis_width, basis_width)
    geometry = jnp.concatenate([coords, area_row, jnp.zeros((4, panels), jnp.float32)], axis=0)
    outgoing = jnp.concatenate([geometry, scaled.astype(jnp.float32)], axis=0)
    blocks = gather_blocks(gather_blocks(outgoing, "ylo"), "core")
    source = blocks.reshape(-1, outgoing.shape[0], panels)
    offdiag, stacked = near_project(
        jnp.transpose(geometry),
        source,
        full_sketch.reshape(probe_count, panels),
        probe_flat,
        tree_order.reshape(panels, 1),
        basis_flat,
    )
    mine = scatter_rows(stacked)
    top = climb_rows(mine, level_mats)
    nested = gather_rows(top).reshape(2, probe_count, basis_width)[None]
    return (offdiag.reshape(probe_count, 1, 1, panels), nested)


def solution(mesh):
    blk = mesh.shape["blk"]
    leaf = mesh.shape["leaf"]
    devices = mesh.devices.reshape(blk // 2, 2, leaf // 8, 2, 2, 2)
    split_mesh = jax.sharding.Mesh(devices, ("ylo", "core", "lz") + LEVEL_AXES[::-1])
    blk_axes = ("ylo", "core")
    leaf_axes = ("lz",) + LEVEL_AXES[::-1]
    in_specs = (
        P(None, leaf_axes, blk_axes, None),
        P(leaf_axes, blk_axes, None),
        P(None, leaf_axes, blk_axes, None),
        P(None, leaf_axes, blk_axes, None),
        P(leaf_axes, blk_axes, None),
        P(leaf_axes, blk_axes, None, None),
        P(leaf_axes, None, None, None),
    )
    out_specs = (P(None, leaf_axes, blk_axes, None), P(leaf_axes, None, None, None))
    return jax.shard_map(
        shards, mesh=split_mesh, in_specs=in_specs, out_specs=out_specs, check_vma=False
    )
```

```python
import math

import jax
import jax.numpy as jnp
from jax import lax
from jax.experimental import pallas as pl
from jax.sharding import PartitionSpec as P

inv_four_pi = 1.0 / (4.0 * math.pi)


def partner(value, axis, bit):
    mask = 2**bit
    pairs = [(source, source ^ mask) for source in range(lax.axis_size(axis))]
    return lax.ppermute(value, axis, pairs)


def kernel_tile(target_pos, target_area, source_pos, source_area):
    distance = jnp.zeros((target_pos.shape[1], source_pos.shape[1]), jnp.float32)
    for component in range(3):
        gap = target_pos[component][:, None] - source_pos[component][None, :]
        distance = distance + gap * gap
    soft = distance + 0.5 * (target_area[:, None] + source_area[None, :])
    return (inv_four_pi * lax.rsqrt(soft)).astype(jnp.bfloat16)


def target_blocks(target_pos, target_area):
    panels = target_pos.shape[1]
    block_size = min(512, panels)
    block_count = panels // block_size
    pos_blocks = jnp.transpose(target_pos.reshape(3, block_count, block_size), (1, 0, 2))
    return (pos_blocks, target_area.reshape(block_count, block_size))


def near_block(target_pos, target_area, source_pos, source_area, source_scaled):
    pos_blocks, area_blocks = target_blocks(target_pos, target_area)

    def one_block(entry):
        block_pos, block_area = entry
        kernel = kernel_tile(block_pos, block_area, source_pos, source_area)
        return lax.dot_general(
            source_scaled, kernel, (((1,), (1,)), ((), ())), preferred_element_type=jnp.float32
        )

    sums = lax.map(one_block, (pos_blocks, area_blocks))
    return jnp.transpose(sums, (1, 0, 2)).reshape(source_scaled.shape[0], target_pos.shape[1])


def project(current, level_mat):
    return jnp.dot(current, level_mat.astype(jnp.float32), precision=lax.Precision.HIGHEST)


LEVEL_AXES = ("lx0", "lx1", "lyhi")


def mirrored(chunks):
    return jnp.where(lax.axis_index("lyhi") == 1, chunks[::-1], chunks)


def climb_rows(rows, level_mats):
    level_count = level_mats.shape[0]
    for tree_level in range(level_count):
        projected = project(rows, level_mats[tree_level])
        if tree_level < level_count - 1:
            other = lax.ppermute(projected, LEVEL_AXES[tree_level], [(0, 1), (1, 0)])
        else:
            count = lax.axis_size("ylo")
            pairs = [
                (chip * 2 + half, (count - 1 - chip) * 2 + 1 - half)
                for chip in range(count)
                for half in range(2)
            ]
            other = lax.ppermute(projected, ("ylo", "lyhi"), pairs)
        rows = projected + other
    return rows


def exchange(value, axis):
    return lax.all_to_all(value, axis, 0, 0, tiled=True)


def gather_blocks(block, axis):
    count = lax.axis_size(axis)
    copies = jnp.broadcast_to(block[None], (count,) + block.shape)
    return exchange(copies.reshape((count * block.shape[0],) + block.shape[1:]), axis)


def scatter_rows(value):
    width = value.shape[1]
    halves = exchange(value, "core").reshape(2, -1, width)
    count = lax.axis_size("ylo")
    summed = mirrored((halves[0] + halves[1]).reshape(count, -1, width))
    return exchange(summed.reshape(-1, width), "ylo").reshape(count, -1, width).sum(axis=0)


def gather_rows(rows):
    count = lax.axis_size("ylo")
    chips = gather_blocks(rows, "ylo").reshape((count,) + rows.shape)
    return gather_blocks(mirrored(chips).reshape(-1, rows.shape[1]), "core")


def near_project_kernel(target_ref, source_ref, sketch_ref, probe_ref, order_ref, basis_ref, off_ref, parts_ref):
    block_count = source_ref.shape[0]
    probe_count, panels = sketch_ref.shape
    geometry_rows = source_ref.shape[1] - probe_count
    target = target_ref[...]
    near = jnp.zeros((probe_count, panels), jnp.float32)
    for block in range(block_count):
        geometry = source_ref[block, 0:geometry_rows, :]
        distance = jnp.zeros((panels, panels), jnp.float32)
        for component in range(3):
            gap = target[:, component : component + 1] - geometry[component : component + 1, :]
            distance = distance + gap * gap
        soft = distance + 0.5 * (target[:, 3:4] + geometry[3:4, :])
        tile = (inv_four_pi * lax.rsqrt(soft)).astype(jnp.bfloat16)
        scaled = source_ref[block, geometry_rows:, :].astype(jnp.bfloat16)
        near = near + lax.dot_general(
            scaled, tile, (((1,), (1,)), ((), ())), preferred_element_type=jnp.float32
        )
    off = (sketch_ref[...].astype(jnp.float32) - near).astype(jnp.bfloat16)
    off_ref[...] = off
    lanes = lax.broadcasted_iota(jnp.int32, (panels, panels), 1)
    onehot = (order_ref[...] == lanes).astype(jnp.bfloat16)
    basis = basis_ref[...]
    for index, values in enumerate((off, probe_ref[...])):
        ordered = lax.dot_general(
            values, onehot, (((1,), (1,)), ((), ())), preferred_element_type=jnp.float32
        ).astype(jnp.bfloat16)
        parts_ref[index * probe_count : (index + 1) * probe_count, :] = jnp.dot(
            ordered, basis, preferred_element_type=jnp.float32
        )


def near_project(target, source, sketch, probe, order, basis):
    probe_count, panels = sketch.shape
    width = basis.shape[1]
    blocks = source.shape[0]
    flops = 2 * probe_count * panels * (blocks * panels + 2 * panels + 2 * width)
    bytes_accessed = 4 * source.size + 2 * (3 * sketch.size + basis.size) + 8 * probe_count * width
    return pl.pallas_call(
        near_project_kernel,
        out_shape=(
            jax.ShapeDtypeStruct((probe_count, panels), jnp.bfloat16),
            jax.ShapeDtypeStruct((2 * probe_count, width), jnp.float32),
        ),
        cost_estimate=pl.CostEstimate(
            flops=flops, transcendentals=blocks * panels * panels, bytes_accessed=bytes_accessed
        ),
    )(target, source, sketch, probe, order, basis)


def shards(positions, panel_areas, probe_cols, full_sketch, tree_order, leaf_basis, transfer_mats):
    panels = positions.shape[3]
    probe_count = probe_cols.shape[0]
    basis_width = leaf_basis.shape[3]
    level_count = transfer_mats.shape[1]
    coords = positions.reshape(3, panels)
    area_row = panel_areas.reshape(1, panels)
    probe_flat = probe_cols.reshape(probe_count, panels)
    scaled = (area_row * probe_flat.astype(jnp.float32)).astype(jnp.bfloat16)
    basis_flat = leaf_basis.reshape(panels, basis_width)
    level_mats = transfer_mats.reshape(level_count, basis_width, basis_width)
    geometry = jnp.concatenate([coords, area_row, jnp.zeros((4, panels), jnp.float32)], axis=0)
    outgoing = jnp.concatenate([geometry, scaled.astype(jnp.float32)], axis=0)
    blocks = gather_blocks(gather_blocks(outgoing, "ylo"), "core")
    source = blocks.reshape(-1, outgoing.shape[0], panels)
    offdiag, stacked = near_project(
        jnp.transpose(geometry),
        source,
        full_sketch.reshape(probe_count, panels),
        probe_flat,
        tree_order.reshape(panels, 1),
        basis_flat,
    )
    mine = scatter_rows(stacked)
    top = climb_rows(mine, level_mats)
    nested = gather_rows(top).reshape(2, probe_count, basis_width)[None]
    return (offdiag.reshape(probe_count, 1, 1, panels), nested)


def solution(mesh):
    blk = mesh.shape["blk"]
    leaf = mesh.shape["leaf"]
    devices = mesh.devices.reshape(blk // 2, 2, leaf // 8, 2, 2, 2)
    split_mesh = jax.sharding.Mesh(devices, ("ylo", "core", "lz") + LEVEL_AXES[::-1])
    blk_axes = ("ylo", "core")
    leaf_axes = ("lz",) + LEVEL_AXES[::-1]
    in_specs = (
        P(None, leaf_axes, blk_axes, None),
        P(leaf_axes, blk_axes, None),
        P(None, leaf_axes, blk_axes, None),
        P(None, leaf_axes, blk_axes, None),
        P(leaf_axes, blk_axes, None),
        P(leaf_axes, blk_axes, None, None),
        P(leaf_axes, None, None, None),
    )
    out_specs = (P(None, leaf_axes, blk_axes, None), P(leaf_axes, None, None, None))
    return jax.shard_map(
        shards, mesh=split_mesh, in_specs=in_specs, out_specs=out_specs, check_vma=False
    )
```

```python
import functools
import math

import jax
import jax.numpy as jnp
from jax import lax
from jax.experimental import pallas as pl
from jax.sharding import PartitionSpec as P

inv_four_pi = 1.0 / (4.0 * math.pi)


def partner(value, axis, bit):
    mask = 2**bit
    pairs = [(source, source ^ mask) for source in range(lax.axis_size(axis))]
    return lax.ppermute(value, axis, pairs)


def kernel_tile(target_pos, target_area, source_pos, source_area):
    distance = jnp.zeros((target_pos.shape[1], source_pos.shape[1]), jnp.float32)
    for component in range(3):
        gap = target_pos[component][:, None] - source_pos[component][None, :]
        distance = distance + gap * gap
    soft = distance + 0.5 * (target_area[:, None] + source_area[None, :])
    return (inv_four_pi * lax.rsqrt(soft)).astype(jnp.bfloat16)


def target_blocks(target_pos, target_area):
    panels = target_pos.shape[1]
    block_size = min(512, panels)
    block_count = panels // block_size
    pos_blocks = jnp.transpose(target_pos.reshape(3, block_count, block_size), (1, 0, 2))
    return (pos_blocks, target_area.reshape(block_count, block_size))


def near_block(target_pos, target_area, source_pos, source_area, source_scaled):
    pos_blocks, area_blocks = target_blocks(target_pos, target_area)

    def one_block(entry):
        block_pos, block_area = entry
        kernel = kernel_tile(block_pos, block_area, source_pos, source_area)
        return lax.dot_general(
            source_scaled, kernel, (((1,), (1,)), ((), ())), preferred_element_type=jnp.float32
        )

    sums = lax.map(one_block, (pos_blocks, area_blocks))
    return jnp.transpose(sums, (1, 0, 2)).reshape(source_scaled.shape[0], target_pos.shape[1])


def project(current, level_mat):
    return jnp.dot(current, level_mat.astype(jnp.float32), precision=lax.Precision.HIGHEST)


LEVEL_AXES = ("lx0", "lx1", "lyhi")


def mirrored(chunks):
    return jnp.where(lax.axis_index("lyhi") == 1, chunks[::-1], chunks)


def climb_rows(rows, level_mats):
    level_count = level_mats.shape[0]
    for tree_level in range(level_count):
        projected = project(rows, level_mats[tree_level])
        if tree_level < level_count - 1:
            other = lax.ppermute(projected, LEVEL_AXES[tree_level], [(0, 1), (1, 0)])
        else:
            count = lax.axis_size("ylo")
            pairs = [
                (chip * 2 + half, (count - 1 - chip) * 2 + 1 - half)
                for chip in range(count)
                for half in range(2)
            ]
            other = lax.ppermute(projected, ("ylo", "lyhi"), pairs)
        rows = projected + other
    return rows


def exchange(value, axis):
    return lax.all_to_all(value, axis, 0, 0, tiled=True)


def gather_blocks(block, axis):
    count = lax.axis_size(axis)
    copies = jnp.broadcast_to(block[None], (count,) + block.shape)
    return exchange(copies.reshape((count * block.shape[0],) + block.shape[1:]), axis)


def scatter_rows(value):
    width = value.shape[1]
    halves = exchange(value, "core").reshape(2, -1, width)
    count = lax.axis_size("ylo")
    summed = mirrored((halves[0] + halves[1]).reshape(count, -1, width))
    return exchange(summed.reshape(-1, width), "ylo").reshape(count, -1, width).sum(axis=0)


def gather_rows(rows):
    count = lax.axis_size("ylo")
    chips = gather_blocks(rows, "ylo").reshape((count,) + rows.shape)
    return gather_blocks(mirrored(chips).reshape(-1, rows.shape[1]), "core")


def chip_kernel(layout, recv_ref, own_ref, full_ref, probe_ref, basis_ref, off_ref, parts_ref):
    blocks_per_core, block_rows, geometry_rows, half = layout
    panels = own_ref.shape[0]
    width = basis_ref.shape[1]
    core = lax.axis_index("core")
    other = 1 - core
    base = blocks_per_core * block_rows
    row0 = pl.multiple_of(core * half, 8)
    lanes = lax.broadcasted_iota(jnp.int32, (panels, panels), 1).astype(jnp.float32)
    targets = (own_ref[...], recv_ref[other, base : base + panels, :])
    sketch_rows = (
        full_ref[pl.ds(row0, half), :].astype(jnp.float32),
        recv_ref[other, base + panels : base + panels + half, :],
    )
    probe_rows = (
        probe_ref[pl.ds(row0, half), :],
        recv_ref[other, base + panels + half : base + panels + 2 * half, :].astype(jnp.bfloat16),
    )
    basis_start = base + panels + 2 * half
    for block in range(2):
        target = targets[block]
        near = jnp.zeros((half, panels), jnp.float32)
        for source_core in range(2):
            for chip in range(blocks_per_core):
                start = chip * block_rows
                geometry = recv_ref[source_core, start : start + geometry_rows, :]
                distance = jnp.zeros((panels, panels), jnp.float32)
                for component in range(3):
                    gap = target[:, component : component + 1] - geometry[component : component + 1, :]
                    distance = distance + gap * gap
                soft = distance + 0.5 * (target[:, 3:4] + geometry[3:4, :])
                tile = (inv_four_pi * lax.rsqrt(soft)).astype(jnp.bfloat16)
                first = pl.multiple_of(start + geometry_rows + row0, 8)
                scaled = recv_ref[source_core, pl.ds(first, half), :].astype(jnp.bfloat16)
                near = near + lax.dot_general(
                    scaled, tile, (((1,), (1,)), ((), ())), preferred_element_type=jnp.float32
                )
        off = (sketch_rows[block] - near).astype(jnp.bfloat16)
        off_ref[block] = off
        onehot = (target[:, 4:5] == lanes).astype(jnp.bfloat16)
        for kind, values in enumerate((off, probe_rows[block])):
            ordered = lax.dot_general(
                values, onehot, (((1,), (1,)), ((), ())), preferred_element_type=jnp.float32
            ).astype(jnp.bfloat16)
            rows = slice(kind * half, (kind + 1) * half)
            if block == 0:
                parts_ref[rows, :] = jnp.dot(
                    ordered, basis_ref[...], preferred_element_type=jnp.float32
                )
            else:
                for quarter in range(width // panels):
                    first = basis_start + quarter * panels
                    basis = recv_ref[other, first : first + panels, :].astype(jnp.bfloat16)
                    columns = slice(quarter * panels, (quarter + 1) * panels)
                    parts_ref[rows, columns] = parts_ref[rows, columns] + jnp.dot(
                        ordered, basis, preferred_element_type=jnp.float32
                    )


def chip_project(layout, recv, own, full, probe, basis):
    probe_count, panels = full.shape
    half = probe_count // 2
    width = basis.shape[1]
    flops = 2 * half * panels * (2 * 2 * layout[0] * panels + 4 * panels + 4 * width)
    bytes_accessed = 4 * recv.size + 2 * (2 * full.size + basis.size) + 4 * probe_count * width
    return pl.pallas_call(
        functools.partial(chip_kernel, layout),
        out_shape=(
            jax.ShapeDtypeStruct((2, half, panels), jnp.bfloat16),
            jax.ShapeDtypeStruct((2 * half, width), jnp.float32),
        ),
        cost_estimate=pl.CostEstimate(
            flops=flops, transcendentals=4 * layout[0] * panels * panels, bytes_accessed=bytes_accessed
        ),
    )(recv, own, full, probe, basis)


def shards(positions, panel_areas, probe_cols, full_sketch, tree_order, leaf_basis, transfer_mats):
    panels = positions.shape[3]
    probe_count = probe_cols.shape[0]
    basis_width = leaf_basis.shape[3]
    level_count = transfer_mats.shape[1]
    half = probe_count // 2
    coords = positions.reshape(3, panels)
    area_row = panel_areas.reshape(1, panels)
    order_row = tree_order.reshape(1, panels).astype(jnp.float32)
    probe_flat = probe_cols.reshape(probe_count, panels)
    full_flat = full_sketch.reshape(probe_count, panels)
    scaled = (area_row * probe_flat.astype(jnp.float32)).astype(jnp.bfloat16)
    basis_flat = leaf_basis.reshape(panels, basis_width)
    level_mats = transfer_mats.reshape(level_count, basis_width, basis_width)
    geometry = jnp.concatenate(
        [coords, area_row, order_row, jnp.zeros((3, panels), jnp.float32)], axis=0
    )
    outgoing = jnp.concatenate([geometry, scaled.astype(jnp.float32)], axis=0)
    chip_blocks = gather_blocks(outgoing, "ylo")
    own = jnp.transpose(geometry)
    own_padded = jnp.pad(own, ((0, 0), (0, panels - own.shape[1])))
    basis_view = jnp.transpose(
        basis_flat.astype(jnp.float32).reshape(panels, basis_width // panels, panels), (1, 0, 2)
    ).reshape(-1, panels)
    full_wide = full_flat.astype(jnp.float32)
    probe_wide = probe_flat.astype(jnp.float32)
    chunks = [
        jnp.concatenate(
            [
                chip_blocks,
                own_padded,
                full_wide[index * half : (index + 1) * half],
                probe_wide[index * half : (index + 1) * half],
                basis_view,
            ],
            axis=0,
        )
        for index in range(2)
    ]
    recv = exchange(jnp.concatenate(chunks, axis=0), "core").reshape(2, -1, panels)
    layout = (lax.axis_size("ylo"), outgoing.shape[0], geometry.shape[0], half)
    off_pair, parts = chip_project(layout, recv, own, full_flat, probe_flat, basis_flat)
    count = lax.axis_size("ylo")
    summed = mirrored(parts.reshape(count, -1, basis_width))
    mine = exchange(summed.reshape(-1, basis_width), "ylo").reshape(count, -1, basis_width).sum(axis=0)
    top = climb_rows(mine, level_mats)
    chips = gather_blocks(top, "ylo").reshape((count,) + top.shape)
    half_rows = mirrored(chips).reshape(-1, basis_width)
    sent_off = off_pair[1].astype(jnp.float32).reshape(-1, basis_width)
    back = gather_blocks(jnp.concatenate([half_rows, sent_off], axis=0), "core")
    back = back.reshape(2, -1, basis_width)
    nested = jnp.stack(
        [
            jnp.concatenate([back[0, :half], back[1, :half]], axis=0),
            jnp.concatenate([back[0, half : 2 * half], back[1, half : 2 * half]], axis=0),
        ],
        axis=0,
    )[None]
    core = lax.axis_index("core")
    received = jnp.where(core == 0, back[1, 2 * half :], back[0, 2 * half :])
    theirs = received.reshape(half, panels).astype(jnp.bfloat16)
    mine_off = off_pair[0]
    offdiag = jnp.where(
        core == 0,
        jnp.concatenate([mine_off, theirs], axis=0),
        jnp.concatenate([theirs, mine_off], axis=0),
    )
    return (offdiag.reshape(probe_count, 1, 1, panels), nested)


def solution(mesh):
    blk = mesh.shape["blk"]
    leaf = mesh.shape["leaf"]
    devices = mesh.devices.reshape(blk // 2, 2, leaf // 8, 2, 2, 2)
    split_mesh = jax.sharding.Mesh(devices, ("ylo", "core", "lz") + LEVEL_AXES[::-1])
    blk_axes = ("ylo", "core")
    leaf_axes = ("lz",) + LEVEL_AXES[::-1]
    in_specs = (
        P(None, leaf_axes, blk_axes, None),
        P(leaf_axes, blk_axes, None),
        P(None, leaf_axes, blk_axes, None),
        P(None, leaf_axes, blk_axes, None),
        P(leaf_axes, blk_axes, None),
        P(leaf_axes, blk_axes, None, None),
        P(leaf_axes, None, None, None),
    )
    out_specs = (P(None, leaf_axes, blk_axes, None), P(leaf_axes, None, None, None))
    return jax.shard_map(
        shards, mesh=split_mesh, in_specs=in_specs, out_specs=out_specs, check_vma=False
    )
```

```python
import functools
import math

import jax
import jax.numpy as jnp
from jax import lax
from jax.experimental import pallas as pl
from jax.sharding import PartitionSpec as P

inv_four_pi = 1.0 / (4.0 * math.pi)


def partner(value, axis, bit):
    mask = 2**bit
    pairs = [(source, source ^ mask) for source in range(lax.axis_size(axis))]
    return lax.ppermute(value, axis, pairs)


def kernel_tile(target_pos, target_area, source_pos, source_area):
    distance = jnp.zeros((target_pos.shape[1], source_pos.shape[1]), jnp.float32)
    for component in range(3):
        gap = target_pos[component][:, None] - source_pos[component][None, :]
        distance = distance + gap * gap
    soft = distance + 0.5 * (target_area[:, None] + source_area[None, :])
    return (inv_four_pi * lax.rsqrt(soft)).astype(jnp.bfloat16)


def target_blocks(target_pos, target_area):
    panels = target_pos.shape[1]
    block_size = min(512, panels)
    block_count = panels // block_size
    pos_blocks = jnp.transpose(target_pos.reshape(3, block_count, block_size), (1, 0, 2))
    return (pos_blocks, target_area.reshape(block_count, block_size))


def near_block(target_pos, target_area, source_pos, source_area, source_scaled):
    pos_blocks, area_blocks = target_blocks(target_pos, target_area)

    def one_block(entry):
        block_pos, block_area = entry
        kernel = kernel_tile(block_pos, block_area, source_pos, source_area)
        return lax.dot_general(
            source_scaled, kernel, (((1,), (1,)), ((), ())), preferred_element_type=jnp.float32
        )

    sums = lax.map(one_block, (pos_blocks, area_blocks))
    return jnp.transpose(sums, (1, 0, 2)).reshape(source_scaled.shape[0], target_pos.shape[1])


def project(current, level_mat):
    return jnp.dot(current, level_mat.astype(jnp.float32), precision=lax.Precision.HIGHEST)


LEVEL_AXES = ("lx0", "lx1", "lyhi")


def mirrored(chunks):
    return jnp.where(lax.axis_index("lyhi") == 1, chunks[::-1], chunks)


def climb_rows(rows, level_mats):
    level_count = level_mats.shape[0]
    for tree_level in range(level_count):
        projected = project(rows, level_mats[tree_level])
        if tree_level < level_count - 1:
            other = lax.ppermute(projected, LEVEL_AXES[tree_level], [(0, 1), (1, 0)])
        else:
            count = lax.axis_size("ylo")
            pairs = [
                (chip * 2 + half, (count - 1 - chip) * 2 + 1 - half)
                for chip in range(count)
                for half in range(2)
            ]
            other = lax.ppermute(projected, ("ylo", "lyhi"), pairs)
        rows = projected + other
    return rows


def exchange(value, axis):
    return lax.all_to_all(value, axis, 0, 0, tiled=True)


def gather_blocks(block, axis):
    count = lax.axis_size(axis)
    copies = jnp.broadcast_to(block[None], (count,) + block.shape)
    return exchange(copies.reshape((count * block.shape[0],) + block.shape[1:]), axis)


def scatter_rows(value):
    width = value.shape[1]
    halves = exchange(value, "core").reshape(2, -1, width)
    count = lax.axis_size("ylo")
    summed = mirrored((halves[0] + halves[1]).reshape(count, -1, width))
    return exchange(summed.reshape(-1, width), "ylo").reshape(count, -1, width).sum(axis=0)


def gather_rows(rows):
    count = lax.axis_size("ylo")
    chips = gather_blocks(rows, "ylo").reshape((count,) + rows.shape)
    return gather_blocks(mirrored(chips).reshape(-1, rows.shape[1]), "core")


def chip_kernel(layout, recv_ref, own_ref, full_ref, probe_ref, basis_ref, off_ref, parts_ref):
    blocks_per_core, block_rows, geometry_rows, half = layout
    panels = own_ref.shape[0]
    width = basis_ref.shape[1]
    core = lax.axis_index("core")
    other = 1 - core
    base = blocks_per_core * block_rows
    row0 = pl.multiple_of(core * half, 8)
    lanes = lax.broadcasted_iota(jnp.int32, (panels, panels), 1).astype(jnp.float32)
    targets = (own_ref[...], recv_ref[other, base : base + panels, :])
    sketch_rows = (
        full_ref[pl.ds(row0, half), :].astype(jnp.float32),
        recv_ref[other, base + panels : base + panels + half, :],
    )
    probe_rows = (
        probe_ref[pl.ds(row0, half), :],
        recv_ref[other, base + panels + half : base + panels + 2 * half, :].astype(jnp.bfloat16),
    )
    basis_start = base + panels + 2 * half
    mirror = lax.axis_index("lyhi")
    pieces = blocks_per_core // 2
    piece_rows = half // pieces
    for block in range(2):
        target = targets[block]
        near = jnp.zeros((half, panels), jnp.float32)
        for source_core in range(2):
            for chip in range(blocks_per_core):
                start = chip * block_rows
                geometry = recv_ref[source_core, start : start + geometry_rows, :]
                distance = jnp.zeros((panels, panels), jnp.float32)
                for component in range(3):
                    gap = target[:, component : component + 1] - geometry[component : component + 1, :]
                    distance = distance + gap * gap
                soft = distance + 0.5 * (target[:, 3:4] + geometry[3:4, :])
                tile = (inv_four_pi * lax.rsqrt(soft)).astype(jnp.bfloat16)
                first = pl.multiple_of(start + geometry_rows + row0, 8)
                scaled = recv_ref[source_core, pl.ds(first, half), :].astype(jnp.bfloat16)
                near = near + lax.dot_general(
                    scaled, tile, (((1,), (1,)), ((), ())), preferred_element_type=jnp.float32
                )
        off = (sketch_rows[block] - near).astype(jnp.bfloat16)
        off_ref[block] = off
        onehot = (target[:, 4:5] == lanes).astype(jnp.bfloat16)
        for kind, values in enumerate((off, probe_rows[block])):
            ordered = lax.dot_general(
                values, onehot, (((1,), (1,)), ((), ())), preferred_element_type=jnp.float32
            ).astype(jnp.bfloat16)
            for sub in range(pieces):
                piece = kind * pieces + sub
                target_piece = piece + mirror * (2 * pieces - 1 - 2 * piece)
                rows = pl.ds(pl.multiple_of(target_piece * piece_rows, 8), piece_rows)
                values_rows = ordered[sub * piece_rows : (sub + 1) * piece_rows]
                if block == 0:
                    parts_ref[rows, :] = jnp.dot(
                        values_rows, basis_ref[...], preferred_element_type=jnp.float32
                    )
                else:
                    for quarter in range(width // panels):
                        first = basis_start + quarter * panels
                        basis = recv_ref[other, first : first + panels, :].astype(jnp.bfloat16)
                        columns = pl.ds(quarter * panels, panels)
                        parts_ref[rows, columns] = parts_ref[rows, columns] + jnp.dot(
                            values_rows, basis, preferred_element_type=jnp.float32
                        )


def chip_project(layout, recv, own, full, probe, basis):
    probe_count, panels = full.shape
    half = probe_count // 2
    width = basis.shape[1]
    flops = 2 * half * panels * (2 * 2 * layout[0] * panels + 4 * panels + 4 * width)
    bytes_accessed = 4 * recv.size + 2 * (2 * full.size + basis.size) + 4 * probe_count * width
    return pl.pallas_call(
        functools.partial(chip_kernel, layout),
        out_shape=(
            jax.ShapeDtypeStruct((2, half, panels), jnp.bfloat16),
            jax.ShapeDtypeStruct((2 * half, width), jnp.float32),
        ),
        cost_estimate=pl.CostEstimate(
            flops=flops, transcendentals=4 * layout[0] * panels * panels, bytes_accessed=bytes_accessed
        ),
    )(recv, own, full, probe, basis)


def shards(positions, panel_areas, probe_cols, full_sketch, tree_order, leaf_basis, transfer_mats):
    panels = positions.shape[3]
    probe_count = probe_cols.shape[0]
    basis_width = leaf_basis.shape[3]
    level_count = transfer_mats.shape[1]
    half = probe_count // 2
    coords = positions.reshape(3, panels)
    area_row = panel_areas.reshape(1, panels)
    order_row = tree_order.reshape(1, panels).astype(jnp.float32)
    probe_flat = probe_cols.reshape(probe_count, panels)
    full_flat = full_sketch.reshape(probe_count, panels)
    scaled = (area_row * probe_flat.astype(jnp.float32)).astype(jnp.bfloat16)
    basis_flat = leaf_basis.reshape(panels, basis_width)
    level_mats = transfer_mats.reshape(level_count, basis_width, basis_width)
    geometry = jnp.concatenate(
        [coords, area_row, order_row, jnp.zeros((3, panels), jnp.float32)], axis=0
    )
    outgoing = jnp.concatenate([geometry, scaled.astype(jnp.float32)], axis=0)
    chip_blocks = gather_blocks(outgoing, "ylo")
    own = jnp.transpose(geometry)
    own_padded = jnp.pad(own, ((0, 0), (0, panels - own.shape[1])))
    basis_view = jnp.transpose(
        basis_flat.astype(jnp.float32).reshape(panels, basis_width // panels, panels), (1, 0, 2)
    ).reshape(-1, panels)
    full_wide = full_flat.astype(jnp.float32)
    probe_wide = probe_flat.astype(jnp.float32)
    chunks = [
        jnp.concatenate(
            [
                chip_blocks,
                own_padded,
                full_wide[index * half : (index + 1) * half],
                probe_wide[index * half : (index + 1) * half],
                basis_view,
            ],
            axis=0,
        )
        for index in range(2)
    ]
    recv = exchange(jnp.concatenate(chunks, axis=0), "core").reshape(2, -1, panels)
    layout = (lax.axis_size("ylo"), outgoing.shape[0], geometry.shape[0], half)
    off_pair, parts = chip_project(layout, recv, own, full_flat, probe_flat, basis_flat)
    count = lax.axis_size("ylo")
    mine = exchange(parts, "ylo").reshape(count, -1, basis_width).sum(axis=0)
    top = climb_rows(mine, level_mats)
    chips = gather_blocks(top, "ylo").reshape((count,) + top.shape)
    half_rows = mirrored(chips).reshape(-1, basis_width)
    sent_off = off_pair[1].astype(jnp.float32).reshape(-1, basis_width)
    back = gather_blocks(jnp.concatenate([half_rows, sent_off], axis=0), "core")
    back = back.reshape(2, -1, basis_width)
    nested = jnp.stack(
        [
            jnp.concatenate([back[0, :half], back[1, :half]], axis=0),
            jnp.concatenate([back[0, half : 2 * half], back[1, half : 2 * half]], axis=0),
        ],
        axis=0,
    )[None]
    core = lax.axis_index("core")
    received = jnp.where(core == 0, back[1, 2 * half :], back[0, 2 * half :])
    theirs = received.reshape(half, panels).astype(jnp.bfloat16)
    mine_off = off_pair[0]
    offdiag = jnp.where(
        core == 0,
        jnp.concatenate([mine_off, theirs], axis=0),
        jnp.concatenate([theirs, mine_off], axis=0),
    )
    return (offdiag.reshape(probe_count, 1, 1, panels), nested)


def solution(mesh):
    blk = mesh.shape["blk"]
    leaf = mesh.shape["leaf"]
    devices = mesh.devices.reshape(blk // 2, 2, leaf // 8, 2, 2, 2)
    split_mesh = jax.sharding.Mesh(devices, ("ylo", "core", "lz") + LEVEL_AXES[::-1])
    blk_axes = ("ylo", "core")
    leaf_axes = ("lz",) + LEVEL_AXES[::-1]
    in_specs = (
        P(None, leaf_axes, blk_axes, None),
        P(leaf_axes, blk_axes, None),
        P(None, leaf_axes, blk_axes, None),
        P(None, leaf_axes, blk_axes, None),
        P(leaf_axes, blk_axes, None),
        P(leaf_axes, blk_axes, None, None),
        P(leaf_axes, None, None, None),
    )
    out_specs = (P(None, leaf_axes, blk_axes, None), P(leaf_axes, None, None, None))
    return jax.shard_map(
        shards, mesh=split_mesh, in_specs=in_specs, out_specs=out_specs, check_vma=False
    )
```

```python
import math

import jax
import jax.numpy as jnp
from jax import lax
from jax.experimental import pallas as pl
from jax.sharding import PartitionSpec as P

inv_four_pi = 1.0 / (4.0 * math.pi)


def partner(value, axis, bit):
    mask = 2**bit
    pairs = [(source, source ^ mask) for source in range(lax.axis_size(axis))]
    return lax.ppermute(value, axis, pairs)


def kernel_tile(target_pos, target_area, source_pos, source_area):
    distance = jnp.zeros((target_pos.shape[1], source_pos.shape[1]), jnp.float32)
    for component in range(3):
        gap = target_pos[component][:, None] - source_pos[component][None, :]
        distance = distance + gap * gap
    soft = distance + 0.5 * (target_area[:, None] + source_area[None, :])
    return (inv_four_pi * lax.rsqrt(soft)).astype(jnp.bfloat16)


def target_blocks(target_pos, target_area):
    panels = target_pos.shape[1]
    block_size = min(512, panels)
    block_count = panels // block_size
    pos_blocks = jnp.transpose(target_pos.reshape(3, block_count, block_size), (1, 0, 2))
    return (pos_blocks, target_area.reshape(block_count, block_size))


def near_block(target_pos, target_area, source_pos, source_area, source_scaled):
    pos_blocks, area_blocks = target_blocks(target_pos, target_area)

    def one_block(entry):
        block_pos, block_area = entry
        kernel = kernel_tile(block_pos, block_area, source_pos, source_area)
        return lax.dot_general(
            source_scaled, kernel, (((1,), (1,)), ((), ())), preferred_element_type=jnp.float32
        )

    sums = lax.map(one_block, (pos_blocks, area_blocks))
    return jnp.transpose(sums, (1, 0, 2)).reshape(source_scaled.shape[0], target_pos.shape[1])


def project(current, level_mat):
    return jnp.dot(current, level_mat.astype(jnp.float32), precision=lax.Precision.HIGHEST)


LEVEL_AXES = ("lx0", "lx1", "lyhi")


def mirrored(chunks):
    return jnp.where(lax.axis_index("lyhi") == 1, chunks[::-1], chunks)


def climb_rows(rows, level_mats):
    for tree_level in range(level_mats.shape[0]):
        projected = project(rows, level_mats[tree_level])
        other = lax.ppermute(projected, LEVEL_AXES[tree_level], [(0, 1), (1, 0)])
        rows = projected + other
    return rows


def ring_shift(rows, sources):
    count = lax.axis_size("ylo")
    ring = 2 * count

    def index(place):
        return (place % count) * 2 + place // count

    pairs = [(index(sources(place) % ring), index(place)) for place in range(ring)]
    return lax.ppermute(rows, ("ylo", "lyhi"), pairs)


def exchange(value, axis):
    return lax.all_to_all(value, axis, 0, 0, tiled=True)


def gather_blocks(block, axis):
    count = lax.axis_size(axis)
    copies = jnp.broadcast_to(block[None], (count,) + block.shape)
    return exchange(copies.reshape((count * block.shape[0],) + block.shape[1:]), axis)


def scatter_rows(value):
    width = value.shape[1]
    halves = exchange(value, "core").reshape(2, -1, width)
    count = lax.axis_size("ylo")
    summed = halves[0] + halves[1]
    return exchange(summed, "ylo").reshape(count, -1, width).sum(axis=0)


def gather_rows(rows):
    count = lax.axis_size("ylo")
    from_left = ring_shift(rows, lambda place: place - 1)
    from_right = ring_shift(rows, lambda place: place + 1)
    far = ring_shift(rows, lambda place: place + 2 if place % 2 == 0 else place - 2)
    by_offset = jnp.stack([rows, from_right, far, from_left], axis=0)
    doubled = jnp.concatenate([by_offset, by_offset], axis=0)
    chip = lax.axis_index("ylo")
    chips = lax.dynamic_slice_in_dim(doubled, (count - chip) % count, count, axis=0)
    return gather_blocks(chips.reshape(-1, rows.shape[1]), "core")


def near_project_kernel(target_ref, source_ref, sketch_ref, probe_ref, order_ref, basis_ref, off_ref, parts_ref):
    block_count = source_ref.shape[0]
    probe_count, panels = sketch_ref.shape
    geometry_rows = source_ref.shape[1] - probe_count
    target = target_ref[...]
    near = jnp.zeros((probe_count, panels), jnp.float32)
    for block in range(block_count):
        geometry = source_ref[block, 0:geometry_rows, :]
        distance = jnp.zeros((panels, panels), jnp.float32)
        for component in range(3):
            gap = target[:, component : component + 1] - geometry[component : component + 1, :]
            distance = distance + gap * gap
        soft = distance + 0.5 * (target[:, 3:4] + geometry[3:4, :])
        tile = (inv_four_pi * lax.rsqrt(soft)).astype(jnp.bfloat16)
        scaled = source_ref[block, geometry_rows:, :].astype(jnp.bfloat16)
        near = near + lax.dot_general(
            scaled, tile, (((1,), (1,)), ((), ())), preferred_element_type=jnp.float32
        )
    off = (sketch_ref[...].astype(jnp.float32) - near).astype(jnp.bfloat16)
    off_ref[...] = off
    lanes = lax.broadcasted_iota(jnp.int32, (panels, panels), 1)
    onehot = (order_ref[...] == lanes).astype(jnp.bfloat16)
    basis = basis_ref[...]
    for index, values in enumerate((off, probe_ref[...])):
        ordered = lax.dot_general(
            values, onehot, (((1,), (1,)), ((), ())), preferred_element_type=jnp.float32
        ).astype(jnp.bfloat16)
        parts_ref[index * probe_count : (index + 1) * probe_count, :] = jnp.dot(
            ordered, basis, preferred_element_type=jnp.float32
        )


def near_project(target, source, sketch, probe, order, basis):
    probe_count, panels = sketch.shape
    width = basis.shape[1]
    blocks = source.shape[0]
    flops = 2 * probe_count * panels * (blocks * panels + 2 * panels + 2 * width)
    bytes_accessed = 4 * source.size + 2 * (3 * sketch.size + basis.size) + 8 * probe_count * width
    return pl.pallas_call(
        near_project_kernel,
        out_shape=(
            jax.ShapeDtypeStruct((probe_count, panels), jnp.bfloat16),
            jax.ShapeDtypeStruct((2 * probe_count, width), jnp.float32),
        ),
        cost_estimate=pl.CostEstimate(
            flops=flops, transcendentals=blocks * panels * panels, bytes_accessed=bytes_accessed
        ),
    )(target, source, sketch, probe, order, basis)


def shards(positions, panel_areas, probe_cols, full_sketch, tree_order, leaf_basis, transfer_mats):
    panels = positions.shape[3]
    probe_count = probe_cols.shape[0]
    basis_width = leaf_basis.shape[3]
    level_count = transfer_mats.shape[1]
    coords = positions.reshape(3, panels)
    area_row = panel_areas.reshape(1, panels)
    probe_flat = probe_cols.reshape(probe_count, panels)
    scaled = (area_row * probe_flat.astype(jnp.float32)).astype(jnp.bfloat16)
    basis_flat = leaf_basis.reshape(panels, basis_width)
    level_mats = transfer_mats.reshape(level_count, basis_width, basis_width)
    geometry = jnp.concatenate([coords, area_row, jnp.zeros((4, panels), jnp.float32)], axis=0)
    outgoing = jnp.concatenate([geometry, scaled.astype(jnp.float32)], axis=0)
    blocks = gather_blocks(gather_blocks(outgoing, "ylo"), "core")
    source = blocks.reshape(-1, outgoing.shape[0], panels)
    offdiag, stacked = near_project(
        jnp.transpose(geometry),
        source,
        full_sketch.reshape(probe_count, panels),
        probe_flat,
        tree_order.reshape(panels, 1),
        basis_flat,
    )
    mine = scatter_rows(stacked)
    top = climb_rows(mine, level_mats)
    nested = gather_rows(top).reshape(2, probe_count, basis_width)[None]
    return (offdiag.reshape(probe_count, 1, 1, panels), nested)


def solution(mesh):
    blk = mesh.shape["blk"]
    leaf = mesh.shape["leaf"]
    devices = mesh.devices.reshape(blk // 2, 2, leaf // 8, 2, 2, 2)
    split_mesh = jax.sharding.Mesh(devices, ("ylo", "core", "lz") + LEVEL_AXES[::-1])
    blk_axes = ("ylo", "core")
    leaf_axes = ("lz",) + LEVEL_AXES[::-1]
    in_specs = (
        P(None, leaf_axes, blk_axes, None),
        P(leaf_axes, blk_axes, None),
        P(None, leaf_axes, blk_axes, None),
        P(None, leaf_axes, blk_axes, None),
        P(leaf_axes, blk_axes, None),
        P(leaf_axes, blk_axes, None, None),
        P(leaf_axes, None, None, None),
    )
    out_specs = (P(None, leaf_axes, blk_axes, None), P(leaf_axes, None, None, None))
    return jax.shard_map(
        shards, mesh=split_mesh, in_specs=in_specs, out_specs=out_specs, check_vma=False
    )
```

```python
import functools
import math

import jax
import jax.numpy as jnp
from jax import lax
from jax.experimental import pallas as pl
from jax.sharding import PartitionSpec as P

inv_four_pi = 1.0 / (4.0 * math.pi)


def partner(value, axis, bit):
    mask = 2**bit
    pairs = [(source, source ^ mask) for source in range(lax.axis_size(axis))]
    return lax.ppermute(value, axis, pairs)


def kernel_tile(target_pos, target_area, source_pos, source_area):
    distance = jnp.zeros((target_pos.shape[1], source_pos.shape[1]), jnp.float32)
    for component in range(3):
        gap = target_pos[component][:, None] - source_pos[component][None, :]
        distance = distance + gap * gap
    soft = distance + 0.5 * (target_area[:, None] + source_area[None, :])
    return (inv_four_pi * lax.rsqrt(soft)).astype(jnp.bfloat16)


def target_blocks(target_pos, target_area):
    panels = target_pos.shape[1]
    block_size = min(512, panels)
    block_count = panels // block_size
    pos_blocks = jnp.transpose(target_pos.reshape(3, block_count, block_size), (1, 0, 2))
    return (pos_blocks, target_area.reshape(block_count, block_size))


def near_block(target_pos, target_area, source_pos, source_area, source_scaled):
    pos_blocks, area_blocks = target_blocks(target_pos, target_area)

    def one_block(entry):
        block_pos, block_area = entry
        kernel = kernel_tile(block_pos, block_area, source_pos, source_area)
        return lax.dot_general(
            source_scaled, kernel, (((1,), (1,)), ((), ())), preferred_element_type=jnp.float32
        )

    sums = lax.map(one_block, (pos_blocks, area_blocks))
    return jnp.transpose(sums, (1, 0, 2)).reshape(source_scaled.shape[0], target_pos.shape[1])


def project(current, level_mat):
    return jnp.dot(current, level_mat.astype(jnp.float32), precision=lax.Precision.HIGHEST)


LEVEL_AXES = ("lx0", "lx1", "lyhi")


def mirrored(chunks):
    return jnp.where(lax.axis_index("lyhi") == 1, chunks[::-1], chunks)


def climb_rows(rows, level_mats):
    for tree_level in range(level_mats.shape[0]):
        projected = project(rows, level_mats[tree_level])
        other = lax.ppermute(projected, LEVEL_AXES[tree_level], [(0, 1), (1, 0)])
        rows = projected + other
    return rows


def ring_shift(rows, sources):
    count = lax.axis_size("ylo")
    ring = 2 * count

    def index(place):
        return (place % count) * 2 + place // count

    pairs = [(index(sources(place) % ring), index(place)) for place in range(ring)]
    return lax.ppermute(rows, ("ylo", "lyhi"), pairs)


def ring_gather(rows):
    count = lax.axis_size("ylo")
    from_left = ring_shift(rows, lambda place: place - 1)
    from_right = ring_shift(rows, lambda place: place + 1)
    far = ring_shift(rows, lambda place: place + 2 if place % 2 == 0 else place - 2)
    by_offset = jnp.stack([rows, from_right, far, from_left], axis=0)
    doubled = jnp.concatenate([by_offset, by_offset], axis=0)
    chip = lax.axis_index("ylo")
    return lax.dynamic_slice_in_dim(doubled, (count - chip) % count, count, axis=0)


def exchange(value, axis):
    return lax.all_to_all(value, axis, 0, 0, tiled=True)


def gather_blocks(block, axis):
    count = lax.axis_size(axis)
    copies = jnp.broadcast_to(block[None], (count,) + block.shape)
    return exchange(copies.reshape((count * block.shape[0],) + block.shape[1:]), axis)


def scatter_rows(value):
    width = value.shape[1]
    halves = exchange(value, "core").reshape(2, -1, width)
    count = lax.axis_size("ylo")
    summed = mirrored((halves[0] + halves[1]).reshape(count, -1, width))
    return exchange(summed.reshape(-1, width), "ylo").reshape(count, -1, width).sum(axis=0)


def gather_rows(rows):
    count = lax.axis_size("ylo")
    chips = gather_blocks(rows, "ylo").reshape((count,) + rows.shape)
    return gather_blocks(mirrored(chips).reshape(-1, rows.shape[1]), "core")


def chip_kernel(layout, recv_ref, own_ref, full_ref, probe_ref, basis_ref, off_ref, parts_ref):
    blocks_per_core, block_rows, geometry_rows, half = layout
    panels = own_ref.shape[0]
    width = basis_ref.shape[1]
    core = lax.axis_index("core")
    other = 1 - core
    base = blocks_per_core * block_rows
    row0 = pl.multiple_of(core * half, 8)
    lanes = lax.broadcasted_iota(jnp.int32, (panels, panels), 1).astype(jnp.float32)
    targets = (own_ref[...], recv_ref[other, base : base + panels, :])
    sketch_rows = (
        full_ref[pl.ds(row0, half), :].astype(jnp.float32),
        recv_ref[other, base + panels : base + panels + half, :],
    )
    probe_rows = (
        probe_ref[pl.ds(row0, half), :],
        recv_ref[other, base + panels + half : base + panels + 2 * half, :].astype(jnp.bfloat16),
    )
    basis_start = base + panels + 2 * half
    for block in range(2):
        target = targets[block]
        near = jnp.zeros((half, panels), jnp.float32)
        for source_core in range(2):
            for chip in range(blocks_per_core):
                start = chip * block_rows
                geometry = recv_ref[source_core, start : start + geometry_rows, :]
                distance = jnp.zeros((panels, panels), jnp.float32)
                for component in range(3):
                    gap = target[:, component : component + 1] - geometry[component : component + 1, :]
                    distance = distance + gap * gap
                soft = distance + 0.5 * (target[:, 3:4] + geometry[3:4, :])
                tile = (inv_four_pi * lax.rsqrt(soft)).astype(jnp.bfloat16)
                first = pl.multiple_of(start + geometry_rows + row0, 8)
                scaled = recv_ref[source_core, pl.ds(first, half), :].astype(jnp.bfloat16)
                near = near + lax.dot_general(
                    scaled, tile, (((1,), (1,)), ((), ())), preferred_element_type=jnp.float32
                )
        off = (sketch_rows[block] - near).astype(jnp.bfloat16)
        off_ref[block] = off
        onehot = (target[:, 4:5] == lanes).astype(jnp.bfloat16)
        for kind, values in enumerate((off, probe_rows[block])):
            ordered = lax.dot_general(
                values, onehot, (((1,), (1,)), ((), ())), preferred_element_type=jnp.float32
            ).astype(jnp.bfloat16)
            rows = slice(kind * half, (kind + 1) * half)
            if block == 0:
                parts_ref[rows, :] = jnp.dot(
                    ordered, basis_ref[...], preferred_element_type=jnp.float32
                )
            else:
                for quarter in range(width // panels):
                    first = basis_start + quarter * panels
                    basis = recv_ref[other, first : first + panels, :].astype(jnp.bfloat16)
                    columns = slice(quarter * panels, (quarter + 1) * panels)
                    parts_ref[rows, columns] = parts_ref[rows, columns] + jnp.dot(
                        ordered, basis, preferred_element_type=jnp.float32
                    )


def chip_project(layout, recv, own, full, probe, basis):
    probe_count, panels = full.shape
    half = probe_count // 2
    width = basis.shape[1]
    flops = 2 * half * panels * (2 * 2 * layout[0] * panels + 4 * panels + 4 * width)
    bytes_accessed = 4 * recv.size + 2 * (2 * full.size + basis.size) + 4 * probe_count * width
    return pl.pallas_call(
        functools.partial(chip_kernel, layout),
        out_shape=(
            jax.ShapeDtypeStruct((2, half, panels), jnp.bfloat16),
            jax.ShapeDtypeStruct((2 * half, width), jnp.float32),
        ),
        cost_estimate=pl.CostEstimate(
            flops=flops, transcendentals=4 * layout[0] * panels * panels, bytes_accessed=bytes_accessed
        ),
    )(recv, own, full, probe, basis)


def shards(positions, panel_areas, probe_cols, full_sketch, tree_order, leaf_basis, transfer_mats):
    panels = positions.shape[3]
    probe_count = probe_cols.shape[0]
    basis_width = leaf_basis.shape[3]
    level_count = transfer_mats.shape[1]
    half = probe_count // 2
    coords = positions.reshape(3, panels)
    area_row = panel_areas.reshape(1, panels)
    order_row = tree_order.reshape(1, panels).astype(jnp.float32)
    probe_flat = probe_cols.reshape(probe_count, panels)
    full_flat = full_sketch.reshape(probe_count, panels)
    scaled = (area_row * probe_flat.astype(jnp.float32)).astype(jnp.bfloat16)
    basis_flat = leaf_basis.reshape(panels, basis_width)
    level_mats = transfer_mats.reshape(level_count, basis_width, basis_width)
    geometry = jnp.concatenate(
        [coords, area_row, order_row, jnp.zeros((3, panels), jnp.float32)], axis=0
    )
    outgoing = jnp.concatenate([geometry, scaled.astype(jnp.float32)], axis=0)
    chip_blocks = gather_blocks(outgoing, "ylo")
    own = jnp.transpose(geometry)
    own_padded = jnp.pad(own, ((0, 0), (0, panels - own.shape[1])))
    basis_view = jnp.transpose(
        basis_flat.astype(jnp.float32).reshape(panels, basis_width // panels, panels), (1, 0, 2)
    ).reshape(-1, panels)
    full_wide = full_flat.astype(jnp.float32)
    probe_wide = probe_flat.astype(jnp.float32)
    chunks = [
        jnp.concatenate(
            [
                chip_blocks,
                own_padded,
                full_wide[index * half : (index + 1) * half],
                probe_wide[index * half : (index + 1) * half],
                basis_view,
            ],
            axis=0,
        )
        for index in range(2)
    ]
    recv = exchange(jnp.concatenate(chunks, axis=0), "core").reshape(2, -1, panels)
    layout = (lax.axis_size("ylo"), outgoing.shape[0], geometry.shape[0], half)
    off_pair, parts = chip_project(layout, recv, own, full_flat, probe_flat, basis_flat)
    count = lax.axis_size("ylo")
    mine = exchange(parts, "ylo").reshape(count, -1, basis_width).sum(axis=0)
    top = climb_rows(mine, level_mats)
    half_rows = ring_gather(top).reshape(-1, basis_width)
    sent_off = off_pair[1].astype(jnp.float32).reshape(-1, basis_width)
    back = gather_blocks(jnp.concatenate([half_rows, sent_off], axis=0), "core")
    back = back.reshape(2, -1, basis_width)
    nested = jnp.stack(
        [
            jnp.concatenate([back[0, :half], back[1, :half]], axis=0),
            jnp.concatenate([back[0, half : 2 * half], back[1, half : 2 * half]], axis=0),
        ],
        axis=0,
    )[None]
    core = lax.axis_index("core")
    received = jnp.where(core == 0, back[1, 2 * half :], back[0, 2 * half :])
    theirs = received.reshape(half, panels).astype(jnp.bfloat16)
    mine_off = off_pair[0]
    offdiag = jnp.where(
        core == 0,
        jnp.concatenate([mine_off, theirs], axis=0),
        jnp.concatenate([theirs, mine_off], axis=0),
    )
    return (offdiag.reshape(probe_count, 1, 1, panels), nested)


def solution(mesh):
    blk = mesh.shape["blk"]
    leaf = mesh.shape["leaf"]
    devices = mesh.devices.reshape(blk // 2, 2, leaf // 8, 2, 2, 2)
    split_mesh = jax.sharding.Mesh(devices, ("ylo", "core", "lz") + LEVEL_AXES[::-1])
    blk_axes = ("ylo", "core")
    leaf_axes = ("lz",) + LEVEL_AXES[::-1]
    in_specs = (
        P(None, leaf_axes, blk_axes, None),
        P(leaf_axes, blk_axes, None),
        P(None, leaf_axes, blk_axes, None),
        P(None, leaf_axes, blk_axes, None),
        P(leaf_axes, blk_axes, None),
        P(leaf_axes, blk_axes, None, None),
        P(leaf_axes, None, None, None),
    )
    out_specs = (P(None, leaf_axes, blk_axes, None), P(leaf_axes, None, None, None))
    return jax.shard_map(
        shards, mesh=split_mesh, in_specs=in_specs, out_specs=out_specs, check_vma=False
    )
```

```python
import functools
import math

import jax
import jax.numpy as jnp
from jax import lax
from jax.experimental import pallas as pl
from jax.sharding import PartitionSpec as P

inv_four_pi = 1.0 / (4.0 * math.pi)


def partner(value, axis, bit):
    mask = 2**bit
    pairs = [(source, source ^ mask) for source in range(lax.axis_size(axis))]
    return lax.ppermute(value, axis, pairs)


def kernel_tile(target_pos, target_area, source_pos, source_area):
    distance = jnp.zeros((target_pos.shape[1], source_pos.shape[1]), jnp.float32)
    for component in range(3):
        gap = target_pos[component][:, None] - source_pos[component][None, :]
        distance = distance + gap * gap
    soft = distance + 0.5 * (target_area[:, None] + source_area[None, :])
    return (inv_four_pi * lax.rsqrt(soft)).astype(jnp.bfloat16)


def target_blocks(target_pos, target_area):
    panels = target_pos.shape[1]
    block_size = min(512, panels)
    block_count = panels // block_size
    pos_blocks = jnp.transpose(target_pos.reshape(3, block_count, block_size), (1, 0, 2))
    return (pos_blocks, target_area.reshape(block_count, block_size))


def near_block(target_pos, target_area, source_pos, source_area, source_scaled):
    pos_blocks, area_blocks = target_blocks(target_pos, target_area)

    def one_block(entry):
        block_pos, block_area = entry
        kernel = kernel_tile(block_pos, block_area, source_pos, source_area)
        return lax.dot_general(
            source_scaled, kernel, (((1,), (1,)), ((), ())), preferred_element_type=jnp.float32
        )

    sums = lax.map(one_block, (pos_blocks, area_blocks))
    return jnp.transpose(sums, (1, 0, 2)).reshape(source_scaled.shape[0], target_pos.shape[1])


def project(current, level_mat):
    return jnp.dot(current, level_mat.astype(jnp.float32), precision=lax.Precision.HIGHEST)


LEVEL_AXES = ("lx0", "lx1", "lyhi")


def mirrored(chunks):
    return jnp.where(lax.axis_index("lyhi") == 1, chunks[::-1], chunks)


def climb_rows(rows, level_mats):
    for tree_level in range(level_mats.shape[0]):
        projected = project(rows, level_mats[tree_level])
        other = lax.ppermute(projected, LEVEL_AXES[tree_level], [(0, 1), (1, 0)])
        rows = projected + other
    return rows


def ring_shift(rows, sources):
    count = lax.axis_size("ylo")
    ring = 2 * count

    def index(place):
        return (place % count) * 2 + place // count

    pairs = [(index(sources(place) % ring), index(place)) for place in range(ring)]
    return lax.ppermute(rows, ("ylo", "lyhi"), pairs)


def ring_gather(rows):
    count = lax.axis_size("ylo")
    from_left = ring_shift(rows, lambda place: place - 1)
    from_right = ring_shift(rows, lambda place: place + 1)
    far = ring_shift(rows, lambda place: place + 2 if place % 2 == 0 else place - 2)
    by_offset = jnp.stack([rows, from_right, far, from_left], axis=0)
    doubled = jnp.concatenate([by_offset, by_offset], axis=0)
    chip = lax.axis_index("ylo")
    return lax.dynamic_slice_in_dim(doubled, (count - chip) % count, count, axis=0)


def exchange(value, axis):
    return lax.all_to_all(value, axis, 0, 0, tiled=True)


def gather_blocks(block, axis):
    count = lax.axis_size(axis)
    copies = jnp.broadcast_to(block[None], (count,) + block.shape)
    return exchange(copies.reshape((count * block.shape[0],) + block.shape[1:]), axis)


def scatter_rows(value):
    width = value.shape[1]
    halves = exchange(value, "core").reshape(2, -1, width)
    count = lax.axis_size("ylo")
    summed = mirrored((halves[0] + halves[1]).reshape(count, -1, width))
    return exchange(summed.reshape(-1, width), "ylo").reshape(count, -1, width).sum(axis=0)


def gather_rows(rows):
    count = lax.axis_size("ylo")
    chips = gather_blocks(rows, "ylo").reshape((count,) + rows.shape)
    return gather_blocks(mirrored(chips).reshape(-1, rows.shape[1]), "core")


def chip_kernel(layout, recv_ref, own_ref, full_ref, probe_ref, basis_ref, off_ref, parts_ref):
    blocks_per_core, block_rows, geometry_rows, half = layout
    panels = own_ref.shape[0]
    width = basis_ref.shape[1]
    core = lax.axis_index("core")
    other = 1 - core
    base = blocks_per_core * block_rows
    row0 = pl.multiple_of(core * half, 8)
    lanes = lax.broadcasted_iota(jnp.int32, (panels, panels), 1).astype(jnp.float32)
    targets = (own_ref[...], recv_ref[other, base : base + panels, :])
    sketch_rows = (
        full_ref[pl.ds(row0, half), :].astype(jnp.float32),
        recv_ref[other, base + panels : base + panels + half, :],
    )
    probe_rows = (
        probe_ref[pl.ds(row0, half), :],
        recv_ref[other, base + panels + half : base + panels + 2 * half, :].astype(jnp.bfloat16),
    )
    basis_start = base + panels + 2 * half
    for block in range(2):
        target = targets[block]
        near = jnp.zeros((half, panels), jnp.float32)
        for source_core in range(2):
            for chip in range(blocks_per_core):
                start = chip * block_rows
                geometry = recv_ref[source_core, start : start + geometry_rows, :]
                distance = jnp.zeros((panels, panels), jnp.float32)
                for component in range(3):
                    gap = target[:, component : component + 1] - geometry[component : component + 1, :]
                    distance = distance + gap * gap
                soft = distance + 0.5 * (target[:, 3:4] + geometry[3:4, :])
                tile = (inv_four_pi * lax.rsqrt(soft)).astype(jnp.bfloat16)
                first = pl.multiple_of(start + geometry_rows + row0, 8)
                scaled = recv_ref[source_core, pl.ds(first, half), :].astype(jnp.bfloat16)
                near = near + lax.dot_general(
                    scaled, tile, (((1,), (1,)), ((), ())), preferred_element_type=jnp.float32
                )
        off = (sketch_rows[block] - near).astype(jnp.bfloat16)
        off_ref[block] = off
        onehot = (target[:, 4:5] == lanes).astype(jnp.bfloat16)
        for kind, values in enumerate((off, probe_rows[block])):
            ordered = lax.dot_general(
                values, onehot, (((1,), (1,)), ((), ())), preferred_element_type=jnp.float32
            ).astype(jnp.bfloat16)
            rows = slice(kind * half, (kind + 1) * half)
            if block == 0:
                parts_ref[rows, :] = jnp.dot(
                    ordered, basis_ref[...], preferred_element_type=jnp.float32
                )
            else:
                for quarter in range(width // panels):
                    first = basis_start + quarter * panels
                    basis = recv_ref[other, first : first + panels, :].astype(jnp.bfloat16)
                    columns = slice(quarter * panels, (quarter + 1) * panels)
                    parts_ref[rows, columns] = parts_ref[rows, columns] + jnp.dot(
                        ordered, basis, preferred_element_type=jnp.float32
                    )


def chip_project(layout, recv, own, full, probe, basis):
    probe_count, panels = full.shape
    half = probe_count // 2
    width = basis.shape[1]
    flops = 2 * half * panels * (2 * 2 * layout[0] * panels + 4 * panels + 4 * width)
    bytes_accessed = 4 * recv.size + 2 * (2 * full.size + basis.size) + 4 * probe_count * width
    return pl.pallas_call(
        functools.partial(chip_kernel, layout),
        out_shape=(
            jax.ShapeDtypeStruct((2, half, panels), jnp.bfloat16),
            jax.ShapeDtypeStruct((2 * half, width), jnp.float32),
        ),
        cost_estimate=pl.CostEstimate(
            flops=flops, transcendentals=4 * layout[0] * panels * panels, bytes_accessed=bytes_accessed
        ),
    )(recv, own, full, probe, basis)


def shards(positions, panel_areas, probe_cols, full_sketch, tree_order, leaf_basis, transfer_mats):
    panels = positions.shape[3]
    probe_count = probe_cols.shape[0]
    basis_width = leaf_basis.shape[3]
    level_count = transfer_mats.shape[1]
    half = probe_count // 2
    coords = positions.reshape(3, panels)
    area_row = panel_areas.reshape(1, panels)
    order_row = tree_order.reshape(1, panels).astype(jnp.float32)
    probe_flat = probe_cols.reshape(probe_count, panels)
    full_flat = full_sketch.reshape(probe_count, panels)
    scaled = (area_row * probe_flat.astype(jnp.float32)).astype(jnp.bfloat16)
    basis_flat = leaf_basis.reshape(panels, basis_width)
    level_mats = transfer_mats.reshape(level_count, basis_width, basis_width)
    geometry = jnp.concatenate(
        [coords, area_row, order_row, jnp.zeros((3, panels), jnp.float32)], axis=0
    )
    outgoing = jnp.concatenate([geometry, scaled.astype(jnp.float32)], axis=0)
    chip_blocks = gather_blocks(outgoing, "ylo")
    own = jnp.transpose(geometry)
    own_padded = jnp.pad(own, ((0, 0), (0, panels - own.shape[1])))
    basis_view = jnp.transpose(
        basis_flat.astype(jnp.float32).reshape(panels, basis_width // panels, panels), (1, 0, 2)
    ).reshape(-1, panels)
    full_wide = full_flat.astype(jnp.float32)
    probe_wide = probe_flat.astype(jnp.float32)
    chunks = [
        jnp.concatenate(
            [
                chip_blocks,
                own_padded,
                full_wide[index * half : (index + 1) * half],
                probe_wide[index * half : (index + 1) * half],
                basis_view,
            ],
            axis=0,
        )
        for index in range(2)
    ]
    recv = exchange(jnp.concatenate(chunks, axis=0), "core").reshape(2, -1, panels)
    layout = (lax.axis_size("ylo"), outgoing.shape[0], geometry.shape[0], half)
    off_pair, parts = chip_project(layout, recv, own, full_flat, probe_flat, basis_flat)
    count = lax.axis_size("ylo")
    chip = lax.axis_index("ylo")
    pieces = parts.reshape(count, -1, basis_width)
    mine = lax.dynamic_index_in_dim(pieces, chip, keepdims=False)
    for step in range(1, count):
        outgoing = lax.dynamic_index_in_dim(pieces, (chip + step) % count, keepdims=False)
        pairs = [(source, (source + step) % count) for source in range(count)]
        mine = mine + lax.ppermute(outgoing, "ylo", pairs)
    top = climb_rows(mine, level_mats)
    half_rows = ring_gather(top).reshape(-1, basis_width)
    sent_off = off_pair[1].astype(jnp.float32).reshape(-1, basis_width)
    back = gather_blocks(jnp.concatenate([half_rows, sent_off], axis=0), "core")
    back = back.reshape(2, -1, basis_width)
    nested = jnp.stack(
        [
            jnp.concatenate([back[0, :half], back[1, :half]], axis=0),
            jnp.concatenate([back[0, half : 2 * half], back[1, half : 2 * half]], axis=0),
        ],
        axis=0,
    )[None]
    core = lax.axis_index("core")
    received = jnp.where(core == 0, back[1, 2 * half :], back[0, 2 * half :])
    theirs = received.reshape(half, panels).astype(jnp.bfloat16)
    mine_off = off_pair[0]
    offdiag = jnp.where(
        core == 0,
        jnp.concatenate([mine_off, theirs], axis=0),
        jnp.concatenate([theirs, mine_off], axis=0),
    )
    return (offdiag.reshape(probe_count, 1, 1, panels), nested)


def solution(mesh):
    blk = mesh.shape["blk"]
    leaf = mesh.shape["leaf"]
    devices = mesh.devices.reshape(blk // 2, 2, leaf // 8, 2, 2, 2)
    split_mesh = jax.sharding.Mesh(devices, ("ylo", "core", "lz") + LEVEL_AXES[::-1])
    blk_axes = ("ylo", "core")
    leaf_axes = ("lz",) + LEVEL_AXES[::-1]
    in_specs = (
        P(None, leaf_axes, blk_axes, None),
        P(leaf_axes, blk_axes, None),
        P(None, leaf_axes, blk_axes, None),
        P(None, leaf_axes, blk_axes, None),
        P(leaf_axes, blk_axes, None),
        P(leaf_axes, blk_axes, None, None),
        P(leaf_axes, None, None, None),
    )
    out_specs = (P(None, leaf_axes, blk_axes, None), P(leaf_axes, None, None, None))
    return jax.shard_map(
        shards, mesh=split_mesh, in_specs=in_specs, out_specs=out_specs, check_vma=False
    )
```

```python
import functools
import math

import jax
import jax.numpy as jnp
from jax import lax
from jax.experimental import pallas as pl
from jax.sharding import PartitionSpec as P

inv_four_pi = 1.0 / (4.0 * math.pi)


def partner(value, axis, bit):
    mask = 2**bit
    pairs = [(source, source ^ mask) for source in range(lax.axis_size(axis))]
    return lax.ppermute(value, axis, pairs)


def kernel_tile(target_pos, target_area, source_pos, source_area):
    distance = jnp.zeros((target_pos.shape[1], source_pos.shape[1]), jnp.float32)
    for component in range(3):
        gap = target_pos[component][:, None] - source_pos[component][None, :]
        distance = distance + gap * gap
    soft = distance + 0.5 * (target_area[:, None] + source_area[None, :])
    return (inv_four_pi * lax.rsqrt(soft)).astype(jnp.bfloat16)


def target_blocks(target_pos, target_area):
    panels = target_pos.shape[1]
    block_size = min(512, panels)
    block_count = panels // block_size
    pos_blocks = jnp.transpose(target_pos.reshape(3, block_count, block_size), (1, 0, 2))
    return (pos_blocks, target_area.reshape(block_count, block_size))


def near_block(target_pos, target_area, source_pos, source_area, source_scaled):
    pos_blocks, area_blocks = target_blocks(target_pos, target_area)

    def one_block(entry):
        block_pos, block_area = entry
        kernel = kernel_tile(block_pos, block_area, source_pos, source_area)
        return lax.dot_general(
            source_scaled, kernel, (((1,), (1,)), ((), ())), preferred_element_type=jnp.float32
        )

    sums = lax.map(one_block, (pos_blocks, area_blocks))
    return jnp.transpose(sums, (1, 0, 2)).reshape(source_scaled.shape[0], target_pos.shape[1])


def project(current, level_mat):
    return jnp.dot(current, level_mat.astype(jnp.float32), precision=lax.Precision.HIGHEST)


LEVEL_AXES = ("lx0", "lx1", "lyhi")


def mirrored(chunks):
    return jnp.where(lax.axis_index("lyhi") == 1, chunks[::-1], chunks)


def climb_rows(rows, level_mats):
    for tree_level in range(level_mats.shape[0]):
        projected = project(rows, level_mats[tree_level])
        other = lax.ppermute(projected, LEVEL_AXES[tree_level], [(0, 1), (1, 0)])
        rows = projected + other
    return rows


def ring_shift(rows, sources):
    count = lax.axis_size("ylo")
    ring = 2 * count

    def index(place):
        return (place % count) * 2 + place // count

    pairs = [(index(sources(place) % ring), index(place)) for place in range(ring)]
    return lax.ppermute(rows, ("ylo", "lyhi"), pairs)


def ring_gather(rows):
    count = lax.axis_size("ylo")
    from_left = ring_shift(rows, lambda place: place - 1)
    from_right = ring_shift(rows, lambda place: place + 1)
    far = ring_shift(rows, lambda place: place + 2 if place % 2 == 0 else place - 2)
    by_offset = jnp.stack([rows, from_right, far, from_left], axis=0)
    doubled = jnp.concatenate([by_offset, by_offset], axis=0)
    chip = lax.axis_index("ylo")
    return lax.dynamic_slice_in_dim(doubled, (count - chip) % count, count, axis=0)


def exchange(value, axis):
    return lax.all_to_all(value, axis, 0, 0, tiled=True)


def gather_blocks(block, axis):
    count = lax.axis_size(axis)
    copies = jnp.broadcast_to(block[None], (count,) + block.shape)
    return exchange(copies.reshape((count * block.shape[0],) + block.shape[1:]), axis)


def scatter_rows(value):
    width = value.shape[1]
    halves = exchange(value, "core").reshape(2, -1, width)
    count = lax.axis_size("ylo")
    summed = mirrored((halves[0] + halves[1]).reshape(count, -1, width))
    return exchange(summed.reshape(-1, width), "ylo").reshape(count, -1, width).sum(axis=0)


def gather_rows(rows):
    count = lax.axis_size("ylo")
    chips = gather_blocks(rows, "ylo").reshape((count,) + rows.shape)
    return gather_blocks(mirrored(chips).reshape(-1, rows.shape[1]), "core")


def chip_kernel(layout, recv_ref, extra_ref, own_ref, full_ref, probe_ref, basis_ref, off_ref, parts_ref):
    blocks_per_core, block_rows, geometry_rows, half = layout
    panels = own_ref.shape[0]
    width = basis_ref.shape[1]
    core = lax.axis_index("core")
    other = 1 - core
    base = blocks_per_core * block_rows
    row0 = pl.multiple_of(core * half, 8)
    lanes = lax.broadcasted_iota(jnp.int32, (panels, panels), 1).astype(jnp.float32)
    targets = (own_ref[...], extra_ref[0:panels, :])
    sketch_rows = (
        full_ref[pl.ds(row0, half), :].astype(jnp.float32),
        extra_ref[panels : panels + half, :],
    )
    probe_rows = (
        probe_ref[pl.ds(row0, half), :],
        extra_ref[panels + half : panels + 2 * half, :].astype(jnp.bfloat16),
    )
    basis_start = panels + 2 * half
    for block in range(2):
        target = targets[block]
        near = jnp.zeros((half, panels), jnp.float32)
        for source_core in range(2):
            for chip in range(blocks_per_core):
                start = chip * block_rows
                geometry = recv_ref[source_core, start : start + geometry_rows, :]
                distance = jnp.zeros((panels, panels), jnp.float32)
                for component in range(3):
                    gap = target[:, component : component + 1] - geometry[component : component + 1, :]
                    distance = distance + gap * gap
                soft = distance + 0.5 * (target[:, 3:4] + geometry[3:4, :])
                tile = (inv_four_pi * lax.rsqrt(soft)).astype(jnp.bfloat16)
                first = pl.multiple_of(start + geometry_rows + row0, 8)
                scaled = recv_ref[source_core, pl.ds(first, half), :].astype(jnp.bfloat16)
                near = near + lax.dot_general(
                    scaled, tile, (((1,), (1,)), ((), ())), preferred_element_type=jnp.float32
                )
        off = (sketch_rows[block] - near).astype(jnp.bfloat16)
        off_ref[block] = off
        onehot = (target[:, 4:5] == lanes).astype(jnp.bfloat16)
        for kind, values in enumerate((off, probe_rows[block])):
            ordered = lax.dot_general(
                values, onehot, (((1,), (1,)), ((), ())), preferred_element_type=jnp.float32
            ).astype(jnp.bfloat16)
            rows = slice(kind * half, (kind + 1) * half)
            if block == 0:
                parts_ref[rows, :] = jnp.dot(
                    ordered, basis_ref[...], preferred_element_type=jnp.float32
                )
            else:
                for quarter in range(width // panels):
                    first = basis_start + quarter * panels
                    basis = extra_ref[first : first + panels, :].astype(jnp.bfloat16)
                    columns = slice(quarter * panels, (quarter + 1) * panels)
                    parts_ref[rows, columns] = parts_ref[rows, columns] + jnp.dot(
                        ordered, basis, preferred_element_type=jnp.float32
                    )


def chip_project(layout, recv, extra, own, full, probe, basis):
    probe_count, panels = full.shape
    half = probe_count // 2
    width = basis.shape[1]
    flops = 2 * half * panels * (2 * 2 * layout[0] * panels + 4 * panels + 4 * width)
    bytes_accessed = 4 * (recv.size + extra.size) + 2 * (2 * full.size + basis.size) + 4 * probe_count * width
    return pl.pallas_call(
        functools.partial(chip_kernel, layout),
        out_shape=(
            jax.ShapeDtypeStruct((2, half, panels), jnp.bfloat16),
            jax.ShapeDtypeStruct((2 * half, width), jnp.float32),
        ),
        cost_estimate=pl.CostEstimate(
            flops=flops, transcendentals=4 * layout[0] * panels * panels, bytes_accessed=bytes_accessed
        ),
    )(recv, extra, own, full, probe, basis)


def shards(positions, panel_areas, probe_cols, full_sketch, tree_order, leaf_basis, transfer_mats):
    panels = positions.shape[3]
    probe_count = probe_cols.shape[0]
    basis_width = leaf_basis.shape[3]
    level_count = transfer_mats.shape[1]
    half = probe_count // 2
    coords = positions.reshape(3, panels)
    area_row = panel_areas.reshape(1, panels)
    order_row = tree_order.reshape(1, panels).astype(jnp.float32)
    probe_flat = probe_cols.reshape(probe_count, panels)
    full_flat = full_sketch.reshape(probe_count, panels)
    scaled = (area_row * probe_flat.astype(jnp.float32)).astype(jnp.bfloat16)
    basis_flat = leaf_basis.reshape(panels, basis_width)
    level_mats = transfer_mats.reshape(level_count, basis_width, basis_width)
    geometry = jnp.concatenate(
        [coords, area_row, order_row, jnp.zeros((3, panels), jnp.float32)], axis=0
    )
    outgoing = jnp.concatenate([geometry, scaled.astype(jnp.float32)], axis=0)
    chip_blocks = gather_blocks(outgoing, "ylo")
    own = jnp.transpose(geometry)
    own_padded = jnp.pad(own, ((0, 0), (0, panels - own.shape[1])))
    basis_view = jnp.transpose(
        basis_flat.astype(jnp.float32).reshape(panels, basis_width // panels, panels), (1, 0, 2)
    ).reshape(-1, panels)
    full_wide = full_flat.astype(jnp.float32)
    probe_wide = probe_flat.astype(jnp.float32)
    other_half = (1 - lax.axis_index("core")) * half
    extra = jnp.concatenate(
        [
            own_padded,
            lax.dynamic_slice_in_dim(full_wide, other_half, half, axis=0),
            lax.dynamic_slice_in_dim(probe_wide, other_half, half, axis=0),
            basis_view,
        ],
        axis=0,
    )
    extra = lax.ppermute(extra, "core", [(0, 1), (1, 0)])
    recv = gather_blocks(chip_blocks, "core").reshape(2, -1, panels)
    layout = (lax.axis_size("ylo"), outgoing.shape[0], geometry.shape[0], half)
    off_pair, parts = chip_project(layout, recv, extra, own, full_flat, probe_flat, basis_flat)
    count = lax.axis_size("ylo")
    mine = exchange(parts, "ylo").reshape(count, -1, basis_width).sum(axis=0)
    top = climb_rows(mine, level_mats)
    half_rows = ring_gather(top).reshape(-1, basis_width)
    sent_off = off_pair[1].astype(jnp.float32).reshape(-1, basis_width)
    back = gather_blocks(jnp.concatenate([half_rows, sent_off], axis=0), "core")
    back = back.reshape(2, -1, basis_width)
    nested = jnp.stack(
        [
            jnp.concatenate([back[0, :half], back[1, :half]], axis=0),
            jnp.concatenate([back[0, half : 2 * half], back[1, half : 2 * half]], axis=0),
        ],
        axis=0,
    )[None]
    core = lax.axis_index("core")
    received = jnp.where(core == 0, back[1, 2 * half :], back[0, 2 * half :])
    theirs = received.reshape(half, panels).astype(jnp.bfloat16)
    mine_off = off_pair[0]
    offdiag = jnp.where(
        core == 0,
        jnp.concatenate([mine_off, theirs], axis=0),
        jnp.concatenate([theirs, mine_off], axis=0),
    )
    return (offdiag.reshape(probe_count, 1, 1, panels), nested)


def solution(mesh):
    blk = mesh.shape["blk"]
    leaf = mesh.shape["leaf"]
    devices = mesh.devices.reshape(blk // 2, 2, leaf // 8, 2, 2, 2)
    split_mesh = jax.sharding.Mesh(devices, ("ylo", "core", "lz") + LEVEL_AXES[::-1])
    blk_axes = ("ylo", "core")
    leaf_axes = ("lz",) + LEVEL_AXES[::-1]
    in_specs = (
        P(None, leaf_axes, blk_axes, None),
        P(leaf_axes, blk_axes, None),
        P(None, leaf_axes, blk_axes, None),
        P(None, leaf_axes, blk_axes, None),
        P(leaf_axes, blk_axes, None),
        P(leaf_axes, blk_axes, None, None),
        P(leaf_axes, None, None, None),
    )
    out_specs = (P(None, leaf_axes, blk_axes, None), P(leaf_axes, None, None, None))
    return jax.shard_map(
        shards, mesh=split_mesh, in_specs=in_specs, out_specs=out_specs, check_vma=False
    )
```

```python
import functools
import math

import jax
import jax.numpy as jnp
from jax import lax
from jax.experimental import pallas as pl
from jax.sharding import PartitionSpec as P

inv_four_pi = 1.0 / (4.0 * math.pi)


def partner(value, axis, bit):
    mask = 2**bit
    pairs = [(source, source ^ mask) for source in range(lax.axis_size(axis))]
    return lax.ppermute(value, axis, pairs)


def kernel_tile(target_pos, target_area, source_pos, source_area):
    distance = jnp.zeros((target_pos.shape[1], source_pos.shape[1]), jnp.float32)
    for component in range(3):
        gap = target_pos[component][:, None] - source_pos[component][None, :]
        distance = distance + gap * gap
    soft = distance + 0.5 * (target_area[:, None] + source_area[None, :])
    return (inv_four_pi * lax.rsqrt(soft)).astype(jnp.bfloat16)


def target_blocks(target_pos, target_area):
    panels = target_pos.shape[1]
    block_size = min(512, panels)
    block_count = panels // block_size
    pos_blocks = jnp.transpose(target_pos.reshape(3, block_count, block_size), (1, 0, 2))
    return (pos_blocks, target_area.reshape(block_count, block_size))


def near_block(target_pos, target_area, source_pos, source_area, source_scaled):
    pos_blocks, area_blocks = target_blocks(target_pos, target_area)

    def one_block(entry):
        block_pos, block_area = entry
        kernel = kernel_tile(block_pos, block_area, source_pos, source_area)
        return lax.dot_general(
            source_scaled, kernel, (((1,), (1,)), ((), ())), preferred_element_type=jnp.float32
        )

    sums = lax.map(one_block, (pos_blocks, area_blocks))
    return jnp.transpose(sums, (1, 0, 2)).reshape(source_scaled.shape[0], target_pos.shape[1])


def project(current, level_mat):
    return jnp.dot(current, level_mat.astype(jnp.float32), precision=lax.Precision.HIGHEST)


LEVEL_AXES = ("lx0", "lx1", "lyhi")


def mirrored(chunks):
    return jnp.where(lax.axis_index("lyhi") == 1, chunks[::-1], chunks)


def climb_rows(rows, level_mats):
    for tree_level in range(level_mats.shape[0]):
        projected = project(rows, level_mats[tree_level])
        other = lax.ppermute(projected, LEVEL_AXES[tree_level], [(0, 1), (1, 0)])
        rows = projected + other
    return rows


def ring_shift(rows, sources):
    count = lax.axis_size("ylo")
    ring = 2 * count

    def index(place):
        return (place % count) * 2 + place // count

    pairs = [(index(sources(place) % ring), index(place)) for place in range(ring)]
    return lax.ppermute(rows, ("ylo", "lyhi"), pairs)


def ring_gather(rows):
    count = lax.axis_size("ylo")
    from_left = ring_shift(rows, lambda place: place - 1)
    from_right = ring_shift(rows, lambda place: place + 1)
    far = ring_shift(rows, lambda place: place + 2 if place % 2 == 0 else place - 2)
    by_offset = jnp.stack([rows, from_right, far, from_left], axis=0)
    doubled = jnp.concatenate([by_offset, by_offset], axis=0)
    chip = lax.axis_index("ylo")
    return lax.dynamic_slice_in_dim(doubled, (count - chip) % count, count, axis=0)


def exchange(value, axis):
    return lax.all_to_all(value, axis, 0, 0, tiled=True)


def gather_blocks(block, axis):
    count = lax.axis_size(axis)
    copies = jnp.broadcast_to(block[None], (count,) + block.shape)
    return exchange(copies.reshape((count * block.shape[0],) + block.shape[1:]), axis)


def scatter_rows(value):
    width = value.shape[1]
    halves = exchange(value, "core").reshape(2, -1, width)
    count = lax.axis_size("ylo")
    summed = mirrored((halves[0] + halves[1]).reshape(count, -1, width))
    return exchange(summed.reshape(-1, width), "ylo").reshape(count, -1, width).sum(axis=0)


def gather_rows(rows):
    count = lax.axis_size("ylo")
    chips = gather_blocks(rows, "ylo").reshape((count,) + rows.shape)
    return gather_blocks(mirrored(chips).reshape(-1, rows.shape[1]), "core")


def chip_kernel(layout, recv_ref, own_ref, full_ref, probe_ref, basis_ref, off_ref, parts_ref):
    blocks_per_core, block_rows, geometry_rows, half = layout
    panels = own_ref.shape[0]
    width = basis_ref.shape[1]
    core = lax.axis_index("core")
    other = 1 - core
    base = blocks_per_core * block_rows
    row0 = pl.multiple_of(core * half, 8)
    lanes = lax.broadcasted_iota(jnp.int32, (panels, panels), 1).astype(jnp.float32)
    targets = (own_ref[...], recv_ref[other, base : base + panels, :])
    sketch_rows = (
        full_ref[pl.ds(row0, half), :].astype(jnp.float32),
        recv_ref[other, base + panels : base + panels + half, :],
    )
    probe_rows = (
        probe_ref[pl.ds(row0, half), :],
        recv_ref[other, base + panels + half : base + panels + 2 * half, :].astype(jnp.bfloat16),
    )
    basis_start = base + panels + 2 * half
    for block in range(2):
        target = targets[block]
        near = jnp.zeros((half, panels), jnp.float32)
        for source_core in range(2):
            for chip in range(blocks_per_core):
                start = chip * block_rows
                geometry = recv_ref[source_core, start : start + geometry_rows, :]
                distance = jnp.zeros((panels, panels), jnp.float32)
                for component in range(3):
                    gap = target[:, component : component + 1] - geometry[component : component + 1, :]
                    distance = distance + gap * gap
                soft = distance + 0.5 * (target[:, 3:4] + geometry[3:4, :])
                tile = (inv_four_pi * lax.rsqrt(soft)).astype(jnp.bfloat16)
                first = pl.multiple_of(start + geometry_rows + row0, 8)
                scaled = recv_ref[source_core, pl.ds(first, half), :].astype(jnp.bfloat16)
                near = near + lax.dot_general(
                    scaled, tile, (((1,), (1,)), ((), ())), preferred_element_type=jnp.float32
                )
        off = (sketch_rows[block] - near).astype(jnp.bfloat16)
        off_ref[block] = off
        onehot = (target[:, 4:5] == lanes).astype(jnp.bfloat16)
        for kind, values in enumerate((off, probe_rows[block])):
            ordered = lax.dot_general(
                values, onehot, (((1,), (1,)), ((), ())), preferred_element_type=jnp.float32
            ).astype(jnp.bfloat16)
            rows = slice(kind * half, (kind + 1) * half)
            if block == 0:
                parts_ref[rows, :] = jnp.dot(
                    ordered, basis_ref[...], preferred_element_type=jnp.float32
                )
            else:
                for quarter in range(width // panels):
                    first = basis_start + quarter * panels
                    basis = recv_ref[other, first : first + panels, :].astype(jnp.bfloat16)
                    columns = slice(quarter * panels, (quarter + 1) * panels)
                    parts_ref[rows, columns] = parts_ref[rows, columns] + jnp.dot(
                        ordered, basis, preferred_element_type=jnp.float32
                    )


def chip_project(layout, recv, own, full, probe, basis):
    probe_count, panels = full.shape
    half = probe_count // 2
    width = basis.shape[1]
    flops = 2 * half * panels * (2 * 2 * layout[0] * panels + 4 * panels + 4 * width)
    bytes_accessed = 4 * recv.size + 2 * (2 * full.size + basis.size) + 4 * probe_count * width
    return pl.pallas_call(
        functools.partial(chip_kernel, layout),
        out_shape=(
            jax.ShapeDtypeStruct((2, half, panels), jnp.bfloat16),
            jax.ShapeDtypeStruct((2 * half, width), jnp.float32),
        ),
        cost_estimate=pl.CostEstimate(
            flops=flops, transcendentals=4 * layout[0] * panels * panels, bytes_accessed=bytes_accessed
        ),
    )(recv, own, full, probe, basis)


def shards(positions, panel_areas, probe_cols, full_sketch, tree_order, leaf_basis, transfer_mats):
    panels = positions.shape[3]
    probe_count = probe_cols.shape[0]
    basis_width = leaf_basis.shape[3]
    level_count = transfer_mats.shape[1]
    half = probe_count // 2
    coords = positions.reshape(3, panels)
    area_row = panel_areas.reshape(1, panels)
    order_row = tree_order.reshape(1, panels).astype(jnp.float32)
    probe_flat = probe_cols.reshape(probe_count, panels)
    full_flat = full_sketch.reshape(probe_count, panels)
    scaled = (area_row * probe_flat.astype(jnp.float32)).astype(jnp.bfloat16)
    basis_flat = leaf_basis.reshape(panels, basis_width)
    level_mats = transfer_mats.reshape(level_count, basis_width, basis_width)
    geometry = jnp.concatenate(
        [coords, area_row, order_row, jnp.zeros((3, panels), jnp.float32)], axis=0
    )
    outgoing = jnp.concatenate([geometry, scaled.astype(jnp.float32)], axis=0)
    chip_count = lax.axis_size("ylo")
    copies = jnp.concatenate(
        [
            jnp.broadcast_to(geometry[None], (chip_count,) + geometry.shape),
            jnp.broadcast_to(scaled[None], (chip_count,) + scaled.shape).astype(jnp.float32),
        ],
        axis=1,
    )
    chip_blocks = exchange(copies.reshape(-1, panels), "ylo")
    own = jnp.transpose(geometry)
    own_padded = jnp.pad(own, ((0, 0), (0, panels - own.shape[1])))
    basis_view = jnp.transpose(
        basis_flat.astype(jnp.float32).reshape(panels, basis_width // panels, panels), (1, 0, 2)
    ).reshape(-1, panels)
    full_wide = full_flat.astype(jnp.float32)
    probe_wide = probe_flat.astype(jnp.float32)
    chunks = [
        jnp.concatenate(
            [
                chip_blocks,
                own_padded,
                full_wide[index * half : (index + 1) * half],
                probe_wide[index * half : (index + 1) * half],
                basis_view,
            ],
            axis=0,
        )
        for index in range(2)
    ]
    recv = exchange(jnp.concatenate(chunks, axis=0), "core").reshape(2, -1, panels)
    layout = (lax.axis_size("ylo"), outgoing.shape[0], geometry.shape[0], half)
    off_pair, parts = chip_project(layout, recv, own, full_flat, probe_flat, basis_flat)
    count = lax.axis_size("ylo")
    mine = exchange(parts, "ylo").reshape(count, -1, basis_width).sum(axis=0)
    top = climb_rows(mine, level_mats)
    half_rows = ring_gather(top).reshape(-1, basis_width)
    sent_off = off_pair[1].astype(jnp.float32).reshape(-1, basis_width)
    back = gather_blocks(jnp.concatenate([half_rows, sent_off], axis=0), "core")
    back = back.reshape(2, -1, basis_width)
    nested = jnp.stack(
        [
            jnp.concatenate([back[0, :half], back[1, :half]], axis=0),
            jnp.concatenate([back[0, half : 2 * half], back[1, half : 2 * half]], axis=0),
        ],
        axis=0,
    )[None]
    core = lax.axis_index("core")
    received = jnp.where(core == 0, back[1, 2 * half :], back[0, 2 * half :])
    theirs = received.reshape(half, panels).astype(jnp.bfloat16)
    mine_off = off_pair[0]
    offdiag = jnp.where(
        core == 0,
        jnp.concatenate([mine_off, theirs], axis=0),
        jnp.concatenate([theirs, mine_off], axis=0),
    )
    return (offdiag.reshape(probe_count, 1, 1, panels), nested)


def solution(mesh):
    blk = mesh.shape["blk"]
    leaf = mesh.shape["leaf"]
    devices = mesh.devices.reshape(blk // 2, 2, leaf // 8, 2, 2, 2)
    split_mesh = jax.sharding.Mesh(devices, ("ylo", "core", "lz") + LEVEL_AXES[::-1])
    blk_axes = ("ylo", "core")
    leaf_axes = ("lz",) + LEVEL_AXES[::-1]
    in_specs = (
        P(None, leaf_axes, blk_axes, None),
        P(leaf_axes, blk_axes, None),
        P(None, leaf_axes, blk_axes, None),
        P(None, leaf_axes, blk_axes, None),
        P(leaf_axes, blk_axes, None),
        P(leaf_axes, blk_axes, None, None),
        P(leaf_axes, None, None, None),
    )
    out_specs = (P(None, leaf_axes, blk_axes, None), P(leaf_axes, None, None, None))
    return jax.shard_map(
        shards, mesh=split_mesh, in_specs=in_specs, out_specs=out_specs, check_vma=False
    )
```
